128 devices in a mesh: group: 4 (over z), local: 32 (over x, y, core).
Axes of the slice: x: 4, y: 4, z: 4, core: 2. Of those that a mesh axis runs over, the one named last changes fastest.
Arguments:
- token_codes: bfloat16 [16384, 3584], P(('group', 'local')), may hold values from -6 to 6
- block_scales: float32 [16384, 28], P(('group', 'local')), may hold values from 0.3 to 3
- route_scores: float32 [16384, 4], P(('group', 'local')), may hold values from -5 to 5
- expert_ids: int32 [16384, 4], P(('group', 'local')), may hold values from 0 to 127, as said below
- w_gate: bfloat16 [128, 3584, 1024], P(('group', 'local')), may hold values from -0.09375 to 0.09375
- w_up: bfloat16 [128, 3584, 1024], P(('group', 'local')), may hold values from -0.09375 to 0.09375
- w_down: bfloat16 [128, 1024, 3584], P(('group', 'local')), may hold values from -0.1875 to 0.1875
- teacher: bfloat16 [16384, 3584], P(('group', 'local')), may hold values from -6 to 6
Outputs:
- student_out: bfloat16 [16384, 3584], P(('group', 'local'))
- grad_tokens: bfloat16 [16384, 3584], P(('group', 'local'))
- grad_scores: float32 [16384, 4], P(('group', 'local'))
The draws below stay inside these ranges and needn't reach their ends.
Inputs may be any that keep to these rules, and one draw needn't show every extreme that they name: `expert_ids`: each row names 4 different experts, all lying in at most 2 of the 4 groups, expert e belonging to group e // 32.
All inputs are finite; a program needn't handle non-finite values.
Results may differ from the reference program's by a relative error of at most 0.022.
Values may be sent and summed in bfloat16 or wider, within the bound.
No kernel may reach another device: no remote copies, remote signals or barrier semaphores. Data moves between devices by JAX's collectives and lax.ppermute only.
A program may use at most 192 MiB of HBM per device.

```python
import math
import jax
import jax.numpy as jnp
from jax import lax

D = 3584
H = 1024
BLOCK = 128
TOPK = 4
TOPG = 2
TOK_DEV = 128
GROUPS = 4
EXP_GROUP = 32
EXPERTS = 128
TOKENS = 16384
CAP = 5
N_GROUP = 4
N_LOCAL = 32
DEVICES = 128


def draw_expert_ids(key, part):
    key_groups, key_bias, key_pick = jax.random.split(key, 3)
    group_order = jax.random.randint(key_groups, (TOKENS, GROUPS), 0, 1 << 16) * GROUPS + jnp.arange(GROUPS, dtype=jnp.int32)
    _, chosen = lax.top_k(group_order, TOPG)
    span = TOPG * EXP_GROUP
    cand_range = jnp.arange(span, dtype=jnp.int32)
    candidates = chosen[:, cand_range // EXP_GROUP] * EXP_GROUP + cand_range % EXP_GROUP
    popular = jax.random.randint(key_bias, (EXPERTS,), 0, 4) * 100
    ranking = (jax.random.randint(key_pick, (TOKENS, span), 0, 1 << 12) + popular[candidates]) * span + cand_range
    _, picked = lax.top_k(ranking, TOPK)
    return jnp.take_along_axis(candidates, picked, axis=1).astype(jnp.int32)


def level_of(key, shape, cuts, smallest, high):
    def one(dim, parts):
        heights = jax.random.uniform(jax.random.fold_in(jax.random.fold_in(key, 6), dim), (parts,), jnp.float32, smallest / len(cuts), high / len(cuts))
        return jnp.repeat(jnp.exp(heights), shape[dim] // parts).reshape((-1,) + (1,) * (len(shape) - dim - 1))

    factor_of = one(*cuts[0])
    for cut in cuts[1:]:
        factor_of = factor_of * one(*cut)
    return factor_of


def gaussian(stream_key, dims, deviation, bound, shards=(), kind=jnp.bfloat16):
    loudness = level_of(stream_key, dims, shards, -0.22, 0.18) if shards else 1.0
    drawn = jax.random.normal(stream_key, dims, jnp.float32) * deviation * loudness
    return jnp.minimum(jnp.maximum(drawn, -bound), bound).astype(kind)


def setup_inputs(seed: int = 0) -> dict:
    key_of = jax.random.split(jax.random.key(seed), 9)
    return {
        "token_codes": gaussian(key_of[0], (TOKENS, D), 1.0, 6.0, ((0, 128),)),
        "block_scales": jnp.clip(jnp.exp(math.log(3.0) - 2.3025851 * jax.random.uniform(key_of[1], (TOKENS, D // BLOCK), jnp.float32) ** level_of(key_of[1], (TOKENS, D // BLOCK), ((0, 128),), -0.2, 0.2)), 0.3, 3.0),
        "route_scores": gaussian(key_of[2], (TOKENS, TOPK), 1.5, 5.0, ((0, 128),), jnp.float32),
        "expert_ids": draw_expert_ids(jax.random.fold_in(key_of[8], 71), 0),
        "w_gate": gaussian(key_of[4], (EXPERTS, D, H), D ** -0.5, 0.09375, ((0, 128),)),
        "w_up": gaussian(key_of[5], (EXPERTS, D, H), D ** -0.5, 0.09375, ((0, 128),)),
        "w_down": gaussian(key_of[6], (EXPERTS, H, D), H ** -0.5, 0.1875, ((0, 128),)),
        "teacher": gaussian(key_of[7], (TOKENS, D), 1.0, 6.0, ((0, 128),)),
    }


CONTRACT_LAST = (((1,), (1,)), ((), ()))


def silu_slope(values):
    gate_sigma = jax.nn.sigmoid(values)
    return gate_sigma * (1.0 + values * (1.0 - gate_sigma))


def expert_pre(in_rows, gate_mat, up_mat):
    pre_gate = jnp.dot(in_rows, gate_mat, preferred_element_type=jnp.float32)
    pre_up = jnp.dot(in_rows, up_mat, preferred_element_type=jnp.float32)
    return pre_gate, pre_up


def expert_out(pre_gate, pre_up, down_mat):
    active = (jax.nn.silu(pre_gate) * pre_up).astype(jnp.bfloat16)
    return jnp.dot(active, down_mat, preferred_element_type=jnp.float32).astype(jnp.bfloat16)


def expert_back(grad_rows, pre_gate, pre_up, gate_mat, up_mat, down_mat):
    grad_act = lax.dot_general(grad_rows, down_mat, CONTRACT_LAST, preferred_element_type=jnp.float32)
    grad_up = (grad_act * jax.nn.silu(pre_gate)).astype(jnp.bfloat16)
    grad_gate = (grad_act * pre_up * silu_slope(pre_gate)).astype(jnp.bfloat16)
    summed = lax.dot_general(grad_gate, gate_mat, CONTRACT_LAST, preferred_element_type=jnp.float32)
    summed = summed + lax.dot_general(grad_up, up_mat, CONTRACT_LAST, preferred_element_type=jnp.float32)
    return summed.astype(jnp.bfloat16)


def reference(token_codes, block_scales, route_scores, expert_ids, w_gate, w_up, w_down, teacher):
    blocks = D // BLOCK
    tokens_x = (token_codes.astype(jnp.float32).reshape(TOKENS, blocks, BLOCK) * block_scales[:, :, None]).reshape(TOKENS, D).astype(jnp.bfloat16)
    gate_sigma = jax.nn.sigmoid(route_scores)
    sigma_sum = jnp.sum(gate_sigma, axis=1, keepdims=True)
    weights = (2.5 * gate_sigma / sigma_sum).astype(jnp.bfloat16)
    weight_flat = weights.reshape(-1).astype(jnp.float32)
    slots_per = DEVICES * CAP
    ids_dev = expert_ids.reshape(DEVICES, TOK_DEV, TOPK)
    expert_range = jnp.arange(EXPERTS, dtype=jnp.int32)
    expert_hits = jnp.zeros((DEVICES, TOK_DEV, EXPERTS), jnp.int32)
    for column in range(TOPK):
        expert_hits = expert_hits + (ids_dev[:, :, column, None] == expert_range).astype(jnp.int32)
    before = jnp.cumsum(expert_hits, axis=1) - expert_hits
    position = jnp.take_along_axis(before, ids_dev, axis=2)
    is_kept = position < CAP
    device_range = jnp.arange(DEVICES, dtype=jnp.int32)[:, None, None]
    slot_index = jnp.where(is_kept, ids_dev * slots_per + device_range * CAP + position, EXPERTS * slots_per)
    slot_codes = jnp.arange(TOKENS * TOPK, dtype=jnp.int32)
    slot_table = jnp.full((EXPERTS * slots_per,), -1, jnp.int32).at[slot_index.reshape(-1)].set(slot_codes, mode="drop")
    slot_table = slot_table.reshape(EXPERTS, slots_per)

    def expert_slice(group_num):
        first_expert = group_num * N_LOCAL
        last_expert = first_expert + N_LOCAL
        return (slot_table[first_expert:last_expert], w_gate[first_expert:last_expert], w_up[first_expert:last_expert], w_down[first_expert:last_expert])

    def unpack(codes_e):
        is_valid = codes_e >= 0
        safe_code = jnp.where(is_valid, codes_e, 0)
        return is_valid, safe_code, safe_code // TOPK

    def forward_visit(running, expert_item):
        codes_e, gate_mat, up_mat, down_mat = expert_item
        is_valid, safe_code, token_pos = unpack(codes_e)
        pre_gate, pre_up = expert_pre(tokens_x[token_pos], gate_mat, up_mat)
        outputs = expert_out(pre_gate, pre_up, down_mat)
        row_scale = jnp.where(is_valid, weight_flat[safe_code], 0.0)
        return running.at[token_pos].add(outputs.astype(jnp.float32) * row_scale[:, None]), None

    combined = jnp.zeros((TOKENS, D), jnp.float32)
    for group_num in range(N_GROUP):
        summed, _ = lax.scan(forward_visit, jnp.zeros((TOKENS, D), jnp.float32), expert_slice(group_num))
        group_part = lax.optimization_barrier(summed.astype(jnp.bfloat16))
        combined = combined + group_part.astype(jnp.float32)
    student_out = combined.astype(jnp.bfloat16)
    grad_y = (student_out.astype(jnp.float32) - teacher.astype(jnp.float32)).astype(jnp.bfloat16)
    upstream = grad_y.astype(jnp.float32)

    def backward_visit(running, expert_item):
        summed, gate_acc = running
        codes_e, gate_mat, up_mat, down_mat = expert_item
        is_valid, safe_code, token_pos = unpack(codes_e)
        pre_gate, pre_up = expert_pre(tokens_x[token_pos], gate_mat, up_mat)
        outputs = expert_out(pre_gate, pre_up, down_mat)
        grad_rows_in = upstream[token_pos]
        gate_terms = jnp.where(is_valid, jnp.sum(grad_rows_in * outputs.astype(jnp.float32), axis=1), 0.0)
        gate_acc = gate_acc.at[safe_code].add(gate_terms)
        row_scale = jnp.where(is_valid, weight_flat[safe_code], 0.0)
        grad_out = (row_scale[:, None] * grad_rows_in).astype(jnp.bfloat16)
        back_rows = expert_back(grad_out, pre_gate, pre_up, gate_mat, up_mat, down_mat)
        summed = summed.at[token_pos].add(back_rows.astype(jnp.float32) * is_valid.astype(jnp.float32)[:, None])
        return (summed, gate_acc), None

    grad_total = jnp.zeros((TOKENS, D), jnp.float32)
    gate_acc = jnp.zeros((TOKENS * TOPK,), jnp.float32)
    for group_num in range(N_GROUP):
        (summed, gate_acc), _ = lax.scan(backward_visit, (jnp.zeros((TOKENS, D), jnp.float32), gate_acc), expert_slice(group_num))
        grad_part = lax.optimization_barrier(summed.astype(jnp.bfloat16))
        grad_total = grad_total + grad_part.astype(jnp.float32)
    grad_tokens = grad_total.astype(jnp.bfloat16)
    grad_w = gate_acc.reshape(TOKENS, TOPK)
    inner_sum = jnp.sum(grad_w * gate_sigma, axis=1, keepdims=True)
    grad_scores = 2.5 * gate_sigma * (1.0 - gate_sigma) * (grad_w / sigma_sum - inner_sum / (sigma_sum * sigma_sum))
    return student_out, grad_tokens, grad_scores
```

```python
import functools
import jax
import jax.numpy as jnp
from jax import lax
from jax.experimental import pallas as pl
from jax.experimental.pallas import tpu as pltpu
from jax.sharding import PartitionSpec as P

T = 128
E = 128
D = 3584
H = 1024
K = 4
CAP = 5
LANE = 128
NB = D // LANE
MAIN = 18
TAIL = NB - MAIN
ROWS = CAP * E
MSG_ROWS = 8 * E
MSG_COLS = MAIN * LANE
GP = 32
GR = GP * 8
F32 = jnp.float32
BF = jnp.bfloat16
NT = (((1,), (1,)), ((), ()))
VMEM_LIMIT = 56 * 1024 * 1024
CHUNKS = ((0, 6), (6, 6), (12, 6))


def cell_of(slot, block):
    index = slot * TAIL + block
    return 5 + index // MAIN, index % MAIN


CELLS = {cell_of(s, b): (s, b) for s in range(CAP) for b in range(TAIL)}


def iota(shape, dim):
    return lax.broadcasted_iota(jnp.int32, shape, dim)


def one_hot(cond):
    return jnp.where(cond, 1.0, 0.0).astype(BF)


def perm_unpack():
    r = iota((GR, GR), 0)
    return one_hot(iota((GR, GR), 1) == (r % GP) * 8 + r // GP)


def perm_pack():
    r = iota((GR, GR), 0)
    return one_hot(iota((GR, GR), 1) == (r % 8) * GP + r // 8)


def unpack(msg_ref, rows_ref):
    perm = perm_unpack()
    for g in range(E // GP):
        for first, count in CHUNKS:
            lanes = slice(first * LANE, (first + count) * LANE)
            moved = jnp.dot(perm, msg_ref[g * GR:(g + 1) * GR, lanes], preferred_element_type=F32).astype(BF)
            for s in range(CAP):
                rows_ref[s * E + g * GP:s * E + (g + 1) * GP, lanes] = moved[s * GP:(s + 1) * GP]
            for q in range(5, 8):
                for c in range(first, first + count):
                    if (q, c) in CELLS:
                        s, b = CELLS[q, c]
                        rows_ref[s * E + g * GP:s * E + (g + 1) * GP, (MAIN + b) * LANE:(MAIN + b + 1) * LANE] = (
                            moved[q * GP:(q + 1) * GP, (c - first) * LANE:(c - first + 1) * LANE]
                        )


def pack(rows_ref, msg_ref):
    perm = perm_pack()
    blank = jnp.zeros((GP, LANE), BF)
    for g in range(E // GP):
        for first, count in CHUNKS:
            lanes = slice(first * LANE, (first + count) * LANE)
            parts = [rows_ref[s * E + g * GP:s * E + (g + 1) * GP, lanes] for s in range(CAP)]
            for q in range(5, 8):
                cells = []
                for c in range(first, first + count):
                    if (q, c) in CELLS:
                        s, b = CELLS[q, c]
                        cells.append(rows_ref[s * E + g * GP:s * E + (g + 1) * GP, (MAIN + b) * LANE:(MAIN + b + 1) * LANE])
                    else:
                        cells.append(blank)
                parts.append(jnp.concatenate(cells, axis=1))
            stacked = jnp.concatenate(parts, axis=0)
            msg_ref[g * GR:(g + 1) * GR, lanes] = jnp.dot(perm, stacked, preferred_element_type=F32).astype(BF)


def slots_of(ids):
    expert = iota((E, T), 0)
    hits = [jnp.where(ids[k:k + 1, :] == expert, 1.0, 0.0) for k in range(K)]
    hit = hits[0] + hits[1] + hits[2] + hits[3]
    earlier = one_hot(iota((T, T), 0) < iota((T, T), 1))
    before = jnp.dot(hit.astype(BF), earlier, preferred_element_type=F32)
    return hits, hit, before


def gates_of(scores):
    sigma = jax.nn.sigmoid(scores)
    total = jnp.sum(sigma, axis=0, keepdims=True)
    return sigma, total


def dispatch_kernel(ids_ref, scales_ref, codes_ref, msg_ref, square, tokens, rows):
    _, hit, before = slots_of(ids_ref[...])
    square[...] = jnp.zeros((LANE, T), F32)
    square[0:NB, :] = scales_ref[...]
    scale = square[...].T
    for j in range(NB):
        lanes = slice(j * LANE, (j + 1) * LANE)
        tokens[:, lanes] = (codes_ref[:, lanes].astype(F32) * scale[:, j:j + 1]).astype(BF)
    for s in range(CAP):
        pick = one_hot((hit > 0.5) & (before == float(s)))
        for n in range(0, D, 512):
            rows[s * E:(s + 1) * E, n:n + 512] = jnp.dot(pick, tokens[:, n:n + 512], preferred_element_type=F32).astype(BF)
    pack(rows, msg_ref)


def table_kernel(ids_ref, scores_ref, spread_ref, mix_ref, sum_ref):
    ids = ids_ref[...]
    hits, hit, before = slots_of(ids)
    sigma, total = gates_of(scores_ref[...])
    weight = (2.5 * sigma / total).astype(BF).astype(F32)
    weighted = hits[0] * weight[0:1]
    for k in range(1, K):
        weighted = weighted + hits[k] * weight[k:k + 1]
    for s in range(CAP):
        here = (hit > 0.5) & (before == float(s))
        spread = jnp.where(here, weighted, 0.0)
        spread_ref[s * E:(s + 1) * E, :] = spread.astype(BF)
        mix_ref[:, s * E:(s + 1) * E] = spread.T.astype(BF)
        sum_ref[:, s * E:(s + 1) * E] = jnp.where(here, 1.0, 0.0).T.astype(BF)


def forward_kernel(msg_ref, gate_ref, up_ref, down_ref, out_ref, pre_gate_ref, pre_up_ref, rows, active):
    step = pl.program_id(0)

    @pl.when(step == 0)
    def _():
        unpack(msg_ref, rows)

    @pl.when(step < 4)
    def _():
        pre_gate = jnp.dot(rows[...], gate_ref[...], preferred_element_type=F32)
        pre_up = jnp.dot(rows[...], up_ref[...], preferred_element_type=F32)
        pre_gate_ref[...] = pre_gate
        pre_up_ref[...] = pre_up
        at = pl.multiple_of(step * 256, 256)
        active[:, pl.ds(at, 256)] = (pre_gate * jax.nn.sigmoid(pre_gate) * pre_up).astype(BF)

    @pl.when(step >= 4)
    def _():
        at = pl.multiple_of((step - 4) * 512, 512)
        rows[:, pl.ds(at, 512)] = jnp.dot(active[...], down_ref[...], preferred_element_type=F32).astype(BF)

    @pl.when(step == 10)
    def _():
        pack(rows, out_ref)


def backward_kernel(msg_ref, pre_gate_ref, pre_up_ref, gate_ref, up_ref, down_ref, out_ref, rows, d_gate, d_up):
    step = pl.program_id(0)

    @pl.when(step == 0)
    def _():
        unpack(msg_ref, rows)

    @pl.when(step < 4)
    def _():
        grad_act = lax.dot_general(rows[...], down_ref[...], NT, preferred_element_type=F32)
        pre_gate = pre_gate_ref[...]
        sig = jax.nn.sigmoid(pre_gate)
        at = pl.multiple_of(step * 256, 256)
        d_up[:, pl.ds(at, 256)] = (grad_act * (pre_gate * sig)).astype(BF)
        d_gate[:, pl.ds(at, 256)] = (grad_act * pre_up_ref[...] * (sig * (1.0 + pre_gate * (1.0 - sig)))).astype(BF)

    @pl.when(step >= 4)
    def _():
        at = pl.multiple_of((step - 4) * 512, 512)
        summed = lax.dot_general(d_gate[...], gate_ref[...], NT, preferred_element_type=F32)
        summed = summed + lax.dot_general(d_up[...], up_ref[...], NT, preferred_element_type=F32)
        rows[:, pl.ds(at, 512)] = summed.astype(BF)

    @pl.when(step == 10)
    def _():
        pack(rows, out_ref)


def combine_kernel(msg_ref, mix_ref, spread_ref, teacher_ref, student_ref, upstream_ref, out_ref, rows):
    unpack(msg_ref, rows)
    for n in range(0, D, 512):
        lanes = slice(n, n + 512)
        student = jnp.dot(mix_ref[...], rows[:, lanes], preferred_element_type=F32).astype(BF)
        student_ref[:, lanes] = student
        upstream = (student.astype(F32) - teacher_ref[:, lanes].astype(F32)).astype(BF)
        upstream_ref[:, lanes] = upstream
    for n in range(0, D, 512):
        lanes = slice(n, n + 512)
        rows[:, lanes] = jnp.dot(spread_ref[...], upstream_ref[:, lanes], preferred_element_type=F32).astype(BF)
    pack(rows, out_ref)


def score_kernel(msg_ref, upstream_ref, ids_ref, scores_ref, out_ref, rows):
    unpack(msg_ref, rows)
    inner = lax.dot_general(rows[...], upstream_ref[...], NT, preferred_element_type=F32)
    hits, hit, before = slots_of(ids_ref[...])
    by_expert = jnp.zeros((E, T), F32)
    for s in range(CAP):
        here = (hit > 0.5) & (before == float(s))
        by_expert = by_expert + jnp.where(here, inner[s * E:(s + 1) * E], 0.0)
    grad_w = jnp.concatenate([jnp.sum(hits[k] * by_expert, axis=0, keepdims=True) for k in range(K)], axis=0)
    sigma, total = gates_of(scores_ref[...])
    inner_sum = jnp.sum(grad_w * sigma, axis=0, keepdims=True)
    out_ref[...] = 2.5 * sigma * (1.0 - sigma) * (grad_w / total - inner_sum / (total * total))


def gather_kernel(msg_ref, sum_ref, out_ref, rows):
    unpack(msg_ref, rows)
    for n in range(0, D, 512):
        lanes = slice(n, n + 512)
        out_ref[:, lanes] = jnp.dot(sum_ref[...], rows[:, lanes], preferred_element_type=F32).astype(BF)


def struct(shape, dtype):
    return jax.ShapeDtypeStruct(shape, dtype)


PARAMS = pltpu.CompilerParams(vmem_limit_bytes=VMEM_LIMIT)
ROWS_SCRATCH = pltpu.VMEM((ROWS, D), BF)
MSG = struct((MSG_ROWS, MSG_COLS), BF)


def cost(flops, moved):
    return pl.CostEstimate(flops=flops, bytes_accessed=moved, transcendentals=0)


def dispatch(ids, scales, codes):
    return pl.pallas_call(
        dispatch_kernel, out_shape=MSG, name="dispatch",
        scratch_shapes=[pltpu.VMEM((LANE, T), F32), pltpu.VMEM((T, D), BF), ROWS_SCRATCH],
        compiler_params=PARAMS, cost_estimate=cost(2 * 10**9, 6 * 10**6),
    )(ids, scales, codes)


def tables(ids, scores):
    return pl.pallas_call(
        table_kernel, name="tables",
        out_shape=(struct((ROWS, T), BF), struct((T, ROWS), BF), struct((T, ROWS), BF)),
        compiler_params=PARAMS, cost_estimate=cost(10**8, 5 * 10**5),
    )(ids, scores)


def whole(shape):
    return pl.BlockSpec(shape, lambda i: (0, 0), pipeline_mode=pl.Buffered(1))


def forward(msg, gate, up, down):
    return pl.pallas_call(
        forward_kernel, name="expert_forward",
        grid=(11,),
        in_specs=[
            whole((MSG_ROWS, MSG_COLS)),
            pl.BlockSpec((D, 256), lambda i: (0, jnp.minimum(i, 3))),
            pl.BlockSpec((D, 256), lambda i: (0, jnp.minimum(i, 3))),
            pl.BlockSpec((H, 512), lambda i: (0, jnp.maximum(i - 4, 0))),
        ],
        out_specs=(
            whole((MSG_ROWS, MSG_COLS)),
            pl.BlockSpec((ROWS, 256), lambda i: (0, jnp.minimum(i, 3))),
            pl.BlockSpec((ROWS, 256), lambda i: (0, jnp.minimum(i, 3))),
        ),
        out_shape=(MSG, struct((ROWS, H), F32), struct((ROWS, H), F32)),
        scratch_shapes=[ROWS_SCRATCH, pltpu.VMEM((ROWS, H), BF)],
        compiler_params=PARAMS, cost_estimate=cost(15 * 10**9, 37 * 10**6),
    )(msg, gate, up, down)


def backward(msg, pre_gate, pre_up, gate, up, down):
    return pl.pallas_call(
        backward_kernel, name="expert_backward",
        grid=(11,),
        in_specs=[
            whole((MSG_ROWS, MSG_COLS)),
            pl.BlockSpec((ROWS, 256), lambda i: (0, jnp.minimum(i, 3))),
            pl.BlockSpec((ROWS, 256), lambda i: (0, jnp.minimum(i, 3))),
            pl.BlockSpec((512, H), lambda i: (jnp.maximum(i - 4, 0), 0)),
            pl.BlockSpec((512, H), lambda i: (jnp.maximum(i - 4, 0), 0)),
            pl.BlockSpec((256, D), lambda i: (jnp.minimum(i, 3), 0)),
        ],
        out_specs=whole((MSG_ROWS, MSG_COLS)),
        out_shape=MSG,
        scratch_shapes=[ROWS_SCRATCH, pltpu.VMEM((ROWS, H), BF), pltpu.VMEM((ROWS, H), BF)],
        compiler_params=PARAMS, cost_estimate=cost(15 * 10**9, 37 * 10**6),
    )(msg, pre_gate, pre_up, gate, up, down)


def combine(msg, mix, spread, teacher):
    return pl.pallas_call(
        combine_kernel, name="combine",
        out_shape=(struct((T, D), BF), struct((T, D), BF), MSG),
        scratch_shapes=[ROWS_SCRATCH],
        compiler_params=PARAMS, cost_estimate=cost(3 * 10**9, 12 * 10**6),
    )(msg, mix, spread, teacher)


def scores_grad(msg, upstream, ids, scores):
    return pl.pallas_call(
        score_kernel, name="scores_grad",
        out_shape=struct((K, T), F32),
        scratch_shapes=[ROWS_SCRATCH],
        compiler_params=PARAMS, cost_estimate=cost(2 * 10**9, 6 * 10**6),
    )(msg, upstream, ids, scores)


def gather(msg, sums):
    return pl.pallas_call(
        gather_kernel, name="gather_tokens",
        out_shape=struct((T, D), BF),
        scratch_shapes=[ROWS_SCRATCH],
        compiler_params=PARAMS, cost_estimate=cost(2 * 10**9, 6 * 10**6),
    )(msg, sums)


def exchange(msg):
    return lax.all_to_all(msg, ("group", "local"), split_axis=0, concat_axis=0, tiled=True)


def per_device(token_codes, block_scales, route_scores, expert_ids, w_gate, w_up, w_down, teacher):
    ids = expert_ids.T
    scores = route_scores.T
    gate, up, down = w_gate[0], w_up[0], w_down[0]
    arrived = exchange(dispatch(ids, block_scales.T, token_codes))
    spread, mix, sums = tables(ids, scores)
    out_msg, pre_gate, pre_up = forward(arrived, gate, up, down)
    returned = exchange(out_msg)
    student_out, upstream, grad_msg = combine(returned, mix, spread, teacher)
    grad_in = exchange(grad_msg)
    grad_scores = scores_grad(returned, upstream, ids, scores)
    grad_back = exchange(backward(grad_in, pre_gate, pre_up, gate, up, down))
    grad_tokens = gather(grad_back, sums)
    return student_out, grad_tokens, grad_scores.T


def solution(mesh):
    rows = P(("group", "local"), None)
    mats = P(("group", "local"), None, None)
    return jax.shard_map(
        per_device, mesh=mesh, in_specs=(rows, rows, rows, rows, mats, mats, mats, rows),
        out_specs=(rows, rows, rows), check_vma=False,
    )
```

```python
import jax
import jax.numpy as jnp
from jax import lax
from jax.experimental import pallas as pl
from jax.experimental.pallas import tpu as pltpu
from jax.sharding import PartitionSpec as P

T = 128
E = 128
D = 3584
H = 1024
K = 4
CAP = 5
LANE = 128
NB = D // LANE
MAIN = 18
TAIL = NB - MAIN
ROWS = CAP * E
MSG_ROWS = 8 * E
MSG_COLS = MAIN * LANE
GP = 32
GR = GP * 8
F32 = jnp.float32
BF = jnp.bfloat16
NT = (((1,), (1,)), ((), ()))
VMEM_LIMIT = 56 * 1024 * 1024
CHUNKS = ((0, 6), (6, 6), (12, 6))
REST = (MAIN, TAIL)
TILES = (REST,) + CHUNKS


def lanes_of(chunk):
    return slice(chunk[0] * LANE, (chunk[0] + chunk[1]) * LANE)


def cell_of(slot, block):
    index = slot * TAIL + block
    return 5 + index // MAIN, index % MAIN


CELLS = {cell_of(s, b): (s, b) for s in range(CAP) for b in range(TAIL)}


def iota(shape, dim):
    return lax.broadcasted_iota(jnp.int32, shape, dim)


def one_hot(cond):
    return jnp.where(cond, 1.0, 0.0).astype(BF)


def perm_unpack():
    r = iota((GR, GR), 0)
    return one_hot(iota((GR, GR), 1) == (r % GP) * 8 + r // GP)


def perm_pack():
    r = iota((GR, GR), 0)
    return one_hot(iota((GR, GR), 1) == (r % 8) * GP + r // 8)


def unpack(msg_ref, rows_ref, perm, chunk):
    first, count = chunk
    lanes = lanes_of(chunk)
    for g in range(E // GP):
        moved = jnp.dot(perm, msg_ref[g * GR:(g + 1) * GR, lanes], preferred_element_type=F32).astype(BF)
        for s in range(CAP):
            rows_ref[s * E + g * GP:s * E + (g + 1) * GP, lanes] = moved[s * GP:(s + 1) * GP]
        for q in range(5, 8):
            for c in range(first, first + count):
                if (q, c) in CELLS:
                    s, b = CELLS[q, c]
                    rows_ref[s * E + g * GP:s * E + (g + 1) * GP, lanes_of((MAIN + b, 1))] = (
                        moved[q * GP:(q + 1) * GP, lanes_of((c - first, 1))]
                    )


def pack(rows_ref, msg_ref, perm, chunk):
    first, count = chunk
    lanes = lanes_of(chunk)
    blank = jnp.zeros((GP, LANE), BF)
    for g in range(E // GP):
        parts = [rows_ref[s * E + g * GP:s * E + (g + 1) * GP, lanes] for s in range(CAP)]
        for q in range(5, 8):
            cells = []
            for c in range(first, first + count):
                if (q, c) in CELLS:
                    s, b = CELLS[q, c]
                    cells.append(rows_ref[s * E + g * GP:s * E + (g + 1) * GP, lanes_of((MAIN + b, 1))])
                else:
                    cells.append(blank)
            parts.append(jnp.concatenate(cells, axis=1))
        stacked = jnp.concatenate(parts, axis=0)
        msg_ref[g * GR:(g + 1) * GR, lanes] = jnp.dot(perm, stacked, preferred_element_type=F32).astype(BF)


class Copies:
    def __init__(self, sems):
        self.sems = sems
        self.used = 0

    def start(self, source, target):
        copy = pltpu.make_async_copy(source, target, self.sems.at[self.used])
        self.used += 1
        copy.start()
        return copy


def wait_all(copies):
    for copy in copies:
        copy.wait()


def slots_of(ids):
    expert = iota((E, T), 0)
    hits = [jnp.where(ids[k:k + 1, :] == expert, 1.0, 0.0) for k in range(K)]
    hit = hits[0] + hits[1] + hits[2] + hits[3]
    earlier = one_hot(iota((T, T), 0) < iota((T, T), 1))
    before = jnp.dot(hit.astype(BF), earlier, preferred_element_type=F32)
    return hits, hit, before


def gates_of(scores):
    sigma = jax.nn.sigmoid(scores)
    total = jnp.sum(sigma, axis=0, keepdims=True)
    return sigma, total


def dispatch_kernel(ids_hbm, scales_hbm, codes_hbm, out_hbm, ids, scales, codes, tokens, rows, msg, sems):
    copies = Copies(sems)
    ids_copy = copies.start(ids_hbm, ids)
    scales_copy = copies.start(scales_hbm, scales.at[0:NB, :])
    code_copies = [copies.start(codes_hbm.at[:, lanes_of(t)], codes.at[:, lanes_of(t)]) for t in TILES]
    perm = perm_pack()
    ids_copy.wait()
    _, hit, before = slots_of(ids[...])
    picks = [one_hot((hit > 0.5) & (before == float(s))) for s in range(CAP)]
    pick = jnp.concatenate(picks, axis=0)
    scales_copy.wait()
    scale = scales[...].T
    sent = []
    for tile, copy in zip(TILES, code_copies):
        copy.wait()
        for j in range(tile[0], tile[0] + tile[1]):
            lanes = lanes_of((j, 1))
            tokens[:, lanes] = (codes[:, lanes].astype(F32) * scale[:, j:j + 1]).astype(BF)
        lanes = lanes_of(tile)
        rows[:, lanes] = jnp.dot(pick, tokens[:, lanes], preferred_element_type=F32).astype(BF)
        if tile is not REST:
            pack(rows, msg, perm, tile)
            sent.append(copies.start(msg.at[:, lanes], out_hbm.at[:, lanes]))
    wait_all(sent)


def table_kernel(ids_ref, scores_ref, spread_ref, mix_ref, sum_ref):
    ids = ids_ref[...]
    hits, hit, before = slots_of(ids)
    sigma, total = gates_of(scores_ref[...])
    weight = (2.5 * sigma / total).astype(BF).astype(F32)
    weighted = hits[0] * weight[0:1]
    for k in range(1, K):
        weighted = weighted + hits[k] * weight[k:k + 1]
    for s in range(CAP):
        here = (hit > 0.5) & (before == float(s))
        spread = jnp.where(here, weighted, 0.0)
        spread_ref[s * E:(s + 1) * E, :] = spread.astype(BF)
        mix_ref[:, s * E:(s + 1) * E] = spread.T.astype(BF)
        sum_ref[:, s * E:(s + 1) * E] = jnp.where(here, 1.0, 0.0).T.astype(BF)


def forward_kernel(
    msg_hbm, gate_hbm, up_hbm, down_hbm, out_hbm, pre_gate_hbm, pre_up_hbm,
    msg, rows, gate, up, down, active, pre_gate_all, pre_up_all, out, sems,
):
    copies = Copies(sems)
    quarter = [slice(n * 256, (n + 1) * 256) for n in range(4)]

    def fetch(n):
        return [
            copies.start(gate_hbm.at[:, quarter[n]], gate.at[:, quarter[n]]),
            copies.start(up_hbm.at[:, quarter[n]], up.at[:, quarter[n]]),
        ]

    def fetch_down(t):
        return [copies.start(down_hbm.at[:, lanes_of(t)], down.at[:, lanes_of(t)])]

    arriving = [copies.start(msg_hbm.at[:, lanes_of(c)], msg.at[:, lanes_of(c)]) for c in CHUNKS]
    coming = [fetch(0)]
    perm = perm_unpack()
    for chunk, copy in zip(CHUNKS, arriving):
        copy.wait()
        unpack(msg, rows, perm, chunk)
        if chunk is CHUNKS[0]:
            coming.append(fetch(1))
    sent = []
    coming_down = []
    for n in range(4):
        wait_all(coming[n])
        if n < 2:
            coming.append(fetch(n + 2))
        else:
            coming_down.extend([fetch_down(TILES[2 * n - 4]), fetch_down(TILES[2 * n - 3])])
        pre_gate = jnp.dot(rows[...], gate[:, quarter[n]], preferred_element_type=F32)
        pre_gate_all[:, quarter[n]] = pre_gate
        pre_up = jnp.dot(rows[...], up[:, quarter[n]], preferred_element_type=F32)
        pre_up_all[:, quarter[n]] = pre_up
        active[:, quarter[n]] = (pre_gate * jax.nn.sigmoid(pre_gate) * pre_up).astype(BF)
        sent.append(copies.start(pre_gate_all.at[:, quarter[n]], pre_gate_hbm.at[:, quarter[n]]))
        sent.append(copies.start(pre_up_all.at[:, quarter[n]], pre_up_hbm.at[:, quarter[n]]))
    perm = perm_pack()
    for tile, coming in zip(TILES, coming_down):
        wait_all(coming)
        lanes = lanes_of(tile)
        rows[:, lanes] = jnp.dot(active[...], down[:, lanes], preferred_element_type=F32).astype(BF)
        if tile is not REST:
            pack(rows, out, perm, tile)
            sent.append(copies.start(out.at[:, lanes], out_hbm.at[:, lanes]))
    wait_all(sent)


def backward_kernel(
    msg_hbm, pre_gate_hbm, pre_up_hbm, gate_hbm, up_hbm, down_hbm, out_hbm,
    msg, rows, both, down, pre_gate_all, pre_up_all, d_both, out, sems,
):
    copies = Copies(sems)
    quarter = [slice(n * 256, (n + 1) * 256) for n in range(4)]

    def fetch(n):
        return [
            copies.start(down_hbm.at[quarter[n], :], down.at[quarter[n], :]),
            copies.start(pre_gate_hbm.at[:, quarter[n]], pre_gate_all.at[:, quarter[n]]),
            copies.start(pre_up_hbm.at[:, quarter[n]], pre_up_all.at[:, quarter[n]]),
        ]

    def fetch_both(t):
        return [
            copies.start(gate_hbm.at[lanes_of(t), :], both.at[lanes_of(t), 0:H]),
            copies.start(up_hbm.at[lanes_of(t), :], both.at[lanes_of(t), H:2 * H]),
        ]

    arriving = [copies.start(msg_hbm.at[:, lanes_of(c)], msg.at[:, lanes_of(c)]) for c in CHUNKS]
    coming = [fetch(0)]
    perm = perm_unpack()
    for chunk, copy in zip(CHUNKS, arriving):
        copy.wait()
        unpack(msg, rows, perm, chunk)
        if chunk is CHUNKS[0]:
            coming.append(fetch(1))
    coming_both = []
    for n in range(4):
        wait_all(coming[n])
        if n < 2:
            coming.append(fetch(n + 2))
        coming_both.append(fetch_both(TILES[n]))
        grad_act = lax.dot_general(rows[...], down[quarter[n], :], NT, preferred_element_type=F32)
        pre_gate = pre_gate_all[:, quarter[n]]
        sig = jax.nn.sigmoid(pre_gate)
        d_both[:, H + n * 256:H + (n + 1) * 256] = (grad_act * (pre_gate * sig)).astype(BF)
        d_both[:, quarter[n]] = (
            grad_act * pre_up_all[:, quarter[n]] * (sig * (1.0 + pre_gate * (1.0 - sig)))
        ).astype(BF)
    perm = perm_pack()
    sent = []
    for tile, coming in zip(TILES, coming_both):
        wait_all(coming)
        lanes = lanes_of(tile)
        rows[:, lanes] = lax.dot_general(d_both[...], both[lanes, :], NT, preferred_element_type=F32).astype(BF)
        if tile is not REST:
            pack(rows, out, perm, tile)
            sent.append(copies.start(out.at[:, lanes], out_hbm.at[:, lanes]))
    wait_all(sent)


def combine_kernel(
    msg_hbm, mix_hbm, spread_hbm, teacher_hbm, student_hbm, upstream_hbm, out_hbm,
    msg, rows, mix, spread, teacher, student, upstream, out, sems,
):
    copies = Copies(sems)
    arriving = [copies.start(msg_hbm.at[:, lanes_of(c)], msg.at[:, lanes_of(c)]) for c in CHUNKS]
    small = [
        copies.start(mix_hbm, mix), copies.start(spread_hbm, spread), copies.start(teacher_hbm, teacher),
    ]
    perm = perm_unpack()
    for chunk, copy in zip(CHUNKS, arriving):
        copy.wait()
        unpack(msg, rows, perm, chunk)
    wait_all(small)
    perm = perm_pack()
    sent = []
    for tile in TILES:
        lanes = lanes_of(tile)
        mixed = jnp.dot(mix[...], rows[:, lanes], preferred_element_type=F32).astype(BF)
        student[:, lanes] = mixed
        upstream[:, lanes] = (mixed.astype(F32) - teacher[:, lanes].astype(F32)).astype(BF)
        rows[:, lanes] = jnp.dot(spread[...], upstream[:, lanes], preferred_element_type=F32).astype(BF)
        if tile is not REST:
            pack(rows, out, perm, tile)
            sent.append(copies.start(out.at[:, lanes], out_hbm.at[:, lanes]))
        if tile is CHUNKS[1]:
            done = slice(0, 12 * LANE)
            sent.append(copies.start(student.at[:, done], student_hbm.at[:, done]))
            sent.append(copies.start(upstream.at[:, done], upstream_hbm.at[:, done]))
    left = slice(12 * LANE, D)
    sent.append(copies.start(student.at[:, left], student_hbm.at[:, left]))
    sent.append(copies.start(upstream.at[:, left], upstream_hbm.at[:, left]))
    wait_all(sent)


def score_kernel(msg_ref, upstream_ref, ids_ref, scores_ref, out_ref, rows):
    perm = perm_unpack()
    for chunk in CHUNKS:
        unpack(msg_ref, rows, perm, chunk)
    inner = lax.dot_general(rows[...], upstream_ref[...], NT, preferred_element_type=F32)
    hits, hit, before = slots_of(ids_ref[...])
    by_expert = jnp.zeros((E, T), F32)
    for s in range(CAP):
        here = (hit > 0.5) & (before == float(s))
        by_expert = by_expert + jnp.where(here, inner[s * E:(s + 1) * E], 0.0)
    grad_w = jnp.concatenate([jnp.sum(hits[k] * by_expert, axis=0, keepdims=True) for k in range(K)], axis=0)
    sigma, total = gates_of(scores_ref[...])
    inner_sum = jnp.sum(grad_w * sigma, axis=0, keepdims=True)
    out_ref[...] = 2.5 * sigma * (1.0 - sigma) * (grad_w / total - inner_sum / (total * total))


def gather_kernel(msg_hbm, sum_hbm, out_hbm, msg, rows, sums, out, sems):
    copies = Copies(sems)
    arriving = [copies.start(msg_hbm.at[:, lanes_of(c)], msg.at[:, lanes_of(c)]) for c in CHUNKS]
    small = copies.start(sum_hbm, sums)
    perm = perm_unpack()
    sent = []
    for chunk, copy in zip(CHUNKS, arriving):
        copy.wait()
        if chunk is CHUNKS[0]:
            small.wait()
        unpack(msg, rows, perm, chunk)
        tiles = (chunk, REST) if chunk is CHUNKS[-1] else (chunk,)
        for tile in tiles:
            lanes = lanes_of(tile)
            out[:, lanes] = jnp.dot(sums[...], rows[:, lanes], preferred_element_type=F32).astype(BF)
            sent.append(copies.start(out.at[:, lanes], out_hbm.at[:, lanes]))
    wait_all(sent)


def struct(shape, dtype):
    return jax.ShapeDtypeStruct(shape, dtype)


PARAMS = pltpu.CompilerParams(vmem_limit_bytes=VMEM_LIMIT)
ROWS_SCRATCH = pltpu.VMEM((ROWS, D), BF)
MSG = struct((MSG_ROWS, MSG_COLS), BF)


def cost(flops, moved):
    return pl.CostEstimate(flops=flops, bytes_accessed=moved, transcendentals=0)


def vmem(shape, dtype=BF):
    return pltpu.VMEM(shape, dtype)


def own(kernel, name, outs, scratch, copies, estimate):
    return pl.pallas_call(
        kernel, name=name, out_shape=outs,
        in_specs=[pl.BlockSpec(memory_space=pl.ANY)] * copies[1],
        out_specs=jax.tree.map(lambda _: pl.BlockSpec(memory_space=pl.ANY), outs),
        scratch_shapes=scratch + [pltpu.SemaphoreType.DMA((copies[0],))],
        compiler_params=PARAMS, cost_estimate=estimate,
    )


MSG_SCRATCH = pltpu.VMEM((MSG_ROWS, MSG_COLS), BF)


def dispatch(ids, scales, codes):
    return own(
        dispatch_kernel, "dispatch", MSG,
        [vmem((K, T), jnp.int32), vmem((LANE, T), F32), vmem((T, D)), vmem((T, D)), ROWS_SCRATCH, MSG_SCRATCH],
        (9, 3), cost(2 * 10**9, 6 * 10**6),
    )(ids, scales, codes)


def tables(ids, scores):
    return pl.pallas_call(
        table_kernel, name="tables",
        out_shape=(struct((ROWS, T), BF), struct((T, ROWS), BF), struct((T, ROWS), BF)),
        compiler_params=PARAMS, cost_estimate=cost(10**8, 5 * 10**5),
    )(ids, scores)


def forward(msg, gate, up, down):
    pre = struct((ROWS, H), F32)
    return own(
        forward_kernel, "expert_forward", (MSG, pre, pre),
        [
            MSG_SCRATCH, ROWS_SCRATCH, vmem((D, H)), vmem((D, H)), vmem((H, D)), vmem((ROWS, H)),
            vmem((ROWS, H), F32), vmem((ROWS, H), F32), MSG_SCRATCH,
        ],
        (26, 4), cost(15 * 10**9, 37 * 10**6),
    )(msg, gate, up, down)


def backward(msg, pre_gate, pre_up, gate, up, down):
    return own(
        backward_kernel, "expert_backward", MSG,
        [
            MSG_SCRATCH, ROWS_SCRATCH, vmem((D, 2 * H)), vmem((H, D)), vmem((ROWS, H), F32), vmem((ROWS, H), F32),
            vmem((ROWS, 2 * H)), MSG_SCRATCH,
        ],
        (26, 6), cost(15 * 10**9, 37 * 10**6),
    )(msg, pre_gate, pre_up, gate, up, down)


def combine(msg, mix, spread, teacher):
    tok = struct((T, D), BF)
    return own(
        combine_kernel, "combine", (tok, tok, MSG),
        [
            MSG_SCRATCH, ROWS_SCRATCH, vmem((T, ROWS)), vmem((ROWS, T)), vmem((T, D)), vmem((T, D)), vmem((T, D)),
            MSG_SCRATCH,
        ],
        (13, 4), cost(3 * 10**9, 12 * 10**6),
    )(msg, mix, spread, teacher)


def scores_grad(msg, upstream, ids, scores):
    return pl.pallas_call(
        score_kernel, name="scores_grad",
        out_shape=struct((K, T), F32),
        scratch_shapes=[ROWS_SCRATCH],
        compiler_params=PARAMS, cost_estimate=cost(2 * 10**9, 6 * 10**6),
    )(msg, upstream, ids, scores)


def gather(msg, sums):
    return own(
        gather_kernel, "gather_tokens", struct((T, D), BF),
        [MSG_SCRATCH, ROWS_SCRATCH, vmem((T, ROWS)), vmem((T, D))],
        (8, 2), cost(2 * 10**9, 6 * 10**6),
    )(msg, sums)


def exchange(msg):
    return lax.all_to_all(msg, ("group", "local"), split_axis=0, concat_axis=0, tiled=True)


def per_device(token_codes, block_scales, route_scores, expert_ids, w_gate, w_up, w_down, teacher):
    ids = expert_ids.T
    scores = route_scores.T
    gate, up, down = w_gate[0], w_up[0], w_down[0]
    arrived = exchange(dispatch(ids, block_scales.T, token_codes))
    spread, mix, sums = tables(ids, scores)
    out_msg, pre_gate, pre_up = forward(arrived, gate, up, down)
    returned = exchange(out_msg)
    student_out, upstream, grad_msg = combine(returned, mix, spread, teacher)
    grad_in = exchange(grad_msg)
    grad_scores = scores_grad(returned, upstream, ids, scores)
    grad_back = exchange(backward(grad_in, pre_gate, pre_up, gate, up, down))
    grad_tokens = gather(grad_back, sums)
    return student_out, grad_tokens, grad_scores.T


def solution(mesh):
    rows = P(("group", "local"), None)
    mats = P(("group", "local"), None, None)
    return jax.shard_map(
        per_device, mesh=mesh, in_specs=(rows, rows, rows, rows, mats, mats, mats, rows),
        out_specs=(rows, rows, rows), check_vma=False,
    )
```

```python
import jax
import jax.numpy as jnp
from jax import lax
from jax.experimental import pallas as pl
from jax.experimental.pallas import tpu as pltpu
from jax.sharding import PartitionSpec as P

T = 128
E = 128
D = 3584
H = 1024
K = 4
CAP = 5
LANE = 128
NB = D // LANE
MAIN = 18
TAIL = NB - MAIN
ROWS = CAP * E
MSG_ROWS = 8 * E
MSG_COLS = MAIN * LANE
GP = 32
GR = GP * 8
F32 = jnp.float32
BF = jnp.bfloat16
NT = (((1,), (1,)), ((), ()))
CHUNKS = ((0, 6), (6, 6), (12, 6))
REST = (MAIN, TAIL)
TILES = (REST,) + CHUNKS


def lanes_of(chunk):
    return slice(chunk[0] * LANE, (chunk[0] + chunk[1]) * LANE)


def cell_of(slot, block):
    index = slot * TAIL + block
    return 5 + index // MAIN, index % MAIN


CELLS = {cell_of(s, b): (s, b) for s in range(CAP) for b in range(TAIL)}


def iota(shape, dim):
    return lax.broadcasted_iota(jnp.int32, shape, dim)


def one_hot(cond):
    return jnp.where(cond, 1.0, 0.0).astype(BF)


def perm_unpack():
    r = iota((GR, GR), 0)
    return one_hot(iota((GR, GR), 1) == (r % GP) * 8 + r // GP)


def perm_pack():
    r = iota((GR, GR), 0)
    return one_hot(iota((GR, GR), 1) == (r % 8) * GP + r // 8)


def unpack(msg_ref, rows_ref, perm, chunk):
    first, count = chunk
    lanes = lanes_of(chunk)
    for g in range(E // GP):
        moved = jnp.dot(perm, msg_ref[g * GR:(g + 1) * GR, lanes], preferred_element_type=F32).astype(BF)
        for s in range(CAP):
            rows_ref[s * E + g * GP:s * E + (g + 1) * GP, lanes] = moved[s * GP:(s + 1) * GP]
        for q in range(5, 8):
            for c in range(first, first + count):
                if (q, c) in CELLS:
                    s, b = CELLS[q, c]
                    rows_ref[s * E + g * GP:s * E + (g + 1) * GP, lanes_of((MAIN + b, 1))] = (
                        moved[q * GP:(q + 1) * GP, lanes_of((c - first, 1))]
                    )


def pack(rows_ref, msg_ref, perm, chunk):
    first, count = chunk
    lanes = lanes_of(chunk)
    blank = jnp.zeros((GP, LANE), BF)
    for g in range(E // GP):
        parts = [rows_ref[s * E + g * GP:s * E + (g + 1) * GP, lanes] for s in range(CAP)]
        for q in range(5, 8):
            cells = []
            for c in range(first, first + count):
                if (q, c) in CELLS:
                    s, b = CELLS[q, c]
                    cells.append(rows_ref[s * E + g * GP:s * E + (g + 1) * GP, lanes_of((MAIN + b, 1))])
                else:
                    cells.append(blank)
            parts.append(jnp.concatenate(cells, axis=1))
        stacked = jnp.concatenate(parts, axis=0)
        msg_ref[g * GR:(g + 1) * GR, lanes] = jnp.dot(perm, stacked, preferred_element_type=F32).astype(BF)


class Copies:
    def __init__(self, sems):
        self.sems = sems
        self.used = 0

    def start(self, source, target):
        copy = pltpu.make_async_copy(source, target, self.sems.at[self.used])
        self.used += 1
        copy.start()
        return copy


def wait_all(copies):
    for copy in copies:
        copy.wait()


def slots_of(ids):
    expert = iota((E, T), 0)
    hits = [jnp.where(ids[k:k + 1, :] == expert, 1.0, 0.0) for k in range(K)]
    hit = hits[0] + hits[1] + hits[2] + hits[3]
    earlier = one_hot(iota((T, T), 0) < iota((T, T), 1))
    before = jnp.dot(hit.astype(BF), earlier, preferred_element_type=F32)
    return hits, hit, before


def gates_of(scores):
    sigma = jax.nn.sigmoid(scores)
    total = jnp.sum(sigma, axis=0, keepdims=True)
    return sigma, total


def dispatch_kernel(
    ids_hbm, scores_hbm, scales_hbm, codes_hbm, msg_ref, spread_ref, mix_ref, sum_ref,
    ids, scores, scales, codes, rows, sems,
):
    copies = Copies(sems)
    ids_copy = copies.start(ids_hbm, ids)
    scales_copy = copies.start(scales_hbm, scales.at[0:NB, :])
    scores_copy = copies.start(scores_hbm, scores)
    code_copies = [copies.start(codes_hbm.at[:, lanes_of(t)], codes.at[:, lanes_of(t)]) for t in TILES]
    perm = perm_pack()
    ids_copy.wait()
    hits, hit, before = slots_of(ids[...])
    here = [(hit > 0.5) & (before == float(s)) for s in range(CAP)]
    pick = jnp.concatenate([one_hot(h) for h in here], axis=0)
    scales_copy.wait()
    scale = scales[...].T
    for tile, copy in zip(TILES, code_copies):
        copy.wait()
        for j in range(tile[0], tile[0] + tile[1]):
            lanes = lanes_of((j, 1))
            codes[:, lanes] = (codes[:, lanes].astype(F32) * scale[:, j:j + 1]).astype(BF)
        lanes = lanes_of(tile)
        rows[:, lanes] = jnp.dot(pick, codes[:, lanes], preferred_element_type=F32).astype(BF)
        if tile is not REST:
            pack(rows, msg_ref, perm, tile)
    scores_copy.wait()
    sigma, total = gates_of(scores[...])
    weight = (2.5 * sigma / total).astype(BF).astype(F32)
    weighted = hits[0] * weight[0:1]
    for k in range(1, K):
        weighted = weighted + hits[k] * weight[k:k + 1]
    for s in range(CAP):
        part = slice(s * E, (s + 1) * E)
        spread = jnp.where(here[s], weighted, 0.0)
        spread_ref[part, :] = spread.astype(BF)
        mix_ref[:, part] = spread.T.astype(BF)
        sum_ref[:, part] = jnp.where(here[s], 1.0, 0.0).T.astype(BF)


def forward_kernel(msg_ref, gate_ref, up_ref, down_ref, out_ref, silu_ref, slope_ref, rows, active):
    perm = perm_unpack()
    for chunk in CHUNKS:
        unpack(msg_ref, rows, perm, chunk)
    for n in range(0, H, 256):
        lanes = slice(n, n + 256)
        pre_gate = jnp.dot(rows[...], gate_ref[:, lanes], preferred_element_type=F32)
        pre_up = jnp.dot(rows[...], up_ref[:, lanes], preferred_element_type=F32)
        sig = jax.nn.sigmoid(pre_gate)
        silu = pre_gate * sig
        active[:, lanes] = (silu * pre_up).astype(BF)
        silu_ref[:, lanes] = silu.astype(BF)
        slope_ref[:, lanes] = (pre_up * (sig * (1.0 + pre_gate * (1.0 - sig)))).astype(BF)
    perm = perm_pack()
    for tile in TILES:
        lanes = lanes_of(tile)
        rows[:, lanes] = jnp.dot(active[...], down_ref[:, lanes], preferred_element_type=F32).astype(BF)
        if tile is not REST:
            pack(rows, out_ref, perm, tile)


def backward_kernel(msg_ref, silu_ref, slope_ref, gate_ref, up_ref, down_ref, out_ref, rows, d_gate, d_up):
    perm = perm_unpack()
    for chunk in CHUNKS:
        unpack(msg_ref, rows, perm, chunk)
    for n in range(0, H, 256):
        lanes = slice(n, n + 256)
        grad_act = lax.dot_general(rows[...], down_ref[lanes, :], NT, preferred_element_type=F32)
        d_up[:, lanes] = (grad_act * silu_ref[:, lanes].astype(F32)).astype(BF)
        d_gate[:, lanes] = (grad_act * slope_ref[:, lanes].astype(F32)).astype(BF)
    perm = perm_pack()
    for tile in TILES:
        lanes = lanes_of(tile)
        summed = lax.dot_general(d_gate[...], gate_ref[lanes, :], NT, preferred_element_type=F32)
        summed = summed + lax.dot_general(d_up[...], up_ref[lanes, :], NT, preferred_element_type=F32)
        rows[:, lanes] = summed.astype(BF)
        if tile is not REST:
            pack(rows, out_ref, perm, tile)


def combine_kernel(
    msg_ref, mix_ref, spread_ref, teacher_ref, ids_ref, scores_ref, student_hbm, grad_scores_ref, out_ref,
    rows, student, inner, sems,
):
    copies = Copies(sems)
    perm = perm_unpack()
    for chunk in CHUNKS:
        unpack(msg_ref, rows, perm, chunk)
    perm = perm_pack()
    sent = []
    for tile in TILES:
        lanes = lanes_of(tile)
        mixed = jnp.dot(mix_ref[...], rows[:, lanes], preferred_element_type=F32).astype(BF)
        student[:, lanes] = mixed
        sent.append(copies.start(student.at[:, lanes], student_hbm.at[:, lanes]))
        upstream = (mixed.astype(F32) - teacher_ref[:, lanes].astype(F32)).astype(BF)
        grad_out = jnp.dot(spread_ref[...], upstream, preferred_element_type=F32)
        product = grad_out * rows[:, lanes].astype(F32)
        partial = product[:, 0:LANE]
        for j in range(1, tile[1]):
            partial = partial + product[:, lanes_of((j, 1))]
        inner[...] = partial if tile is REST else inner[...] + partial
        rows[:, lanes] = grad_out.astype(BF)
        if tile is not REST:
            pack(rows, out_ref, perm, tile)
    slot_inner = jnp.sum(inner[...], axis=1, keepdims=True)
    hits, hit, before = slots_of(ids_ref[...])
    by_expert = jnp.zeros((E, T), F32)
    for s in range(CAP):
        here = (hit > 0.5) & (before == float(s))
        by_expert = by_expert + jnp.where(here, slot_inner[s * E:(s + 1) * E], 0.0)
    sigma, total = gates_of(scores_ref[...])
    weight = (2.5 * sigma / total).astype(BF).astype(F32)
    weighted_inner = jnp.concatenate(
        [jnp.sum(hits[k] * by_expert, axis=0, keepdims=True) for k in range(K)], axis=0
    )
    grad_w = weighted_inner / weight
    inner_sum = jnp.sum(grad_w * sigma, axis=0, keepdims=True)
    grad_scores_ref[...] = 2.5 * sigma * (1.0 - sigma) * (grad_w / total - inner_sum / (total * total))
    wait_all(sent)


def gather_kernel(msg_ref, sum_ref, out_hbm, rows, out, sems):
    copies = Copies(sems)
    perm = perm_unpack()
    sent = []
    for chunk in CHUNKS:
        unpack(msg_ref, rows, perm, chunk)
        tiles = (REST, chunk) if chunk is CHUNKS[-1] else (chunk,)
        for tile in tiles:
            lanes = lanes_of(tile)
            out[:, lanes] = jnp.dot(sum_ref[...], rows[:, lanes], preferred_element_type=F32).astype(BF)
            sent.append(copies.start(out.at[:, lanes], out_hbm.at[:, lanes]))
    wait_all(sent)


def struct(shape, dtype=BF):
    return jax.ShapeDtypeStruct(shape, dtype)


def vmem(shape, dtype=BF):
    return pltpu.VMEM(shape, dtype)


MSG = struct((MSG_ROWS, MSG_COLS))
ROWS_SCRATCH = vmem((ROWS, D))
ON_CHIP = pl.BlockSpec(memory_space=pltpu.VMEM)
IN_HBM = pl.BlockSpec(memory_space=pltpu.HBM)


def on_chip(array):
    return pltpu.with_memory_space_constraint(array, pltpu.VMEM)


def in_hbm(array):
    return pltpu.with_memory_space_constraint(array, pltpu.HBM)


def own(kernel, name, outs, scratch, limit, estimate, in_specs, out_specs):
    return pl.pallas_call(
        kernel, name=name, out_shape=outs, in_specs=in_specs, out_specs=out_specs, scratch_shapes=scratch,
        compiler_params=pltpu.CompilerParams(vmem_limit_bytes=limit * 2**20),
        cost_estimate=pl.CostEstimate(flops=estimate[0], bytes_accessed=estimate[1], transcendentals=0),
    )


def copy_sems(count):
    return pltpu.SemaphoreType.DMA((count,))


HID = struct((ROWS, H))
TOK_HBM = pltpu.HBM((T, D), BF)


def dispatch(ids, scores, scales, codes):
    return own(
        dispatch_kernel, "dispatch", (MSG, struct((ROWS, T)), struct((T, ROWS)), struct((T, ROWS))),
        [vmem((K, T), jnp.int32), vmem((K, T), F32), vmem((LANE, T), F32), vmem((T, D)), ROWS_SCRATCH, copy_sems(7)],
        16, (60 * 10**9, 6 * 10**6), [IN_HBM] * 4, (ON_CHIP,) * 4,
    )(in_hbm(ids), in_hbm(scores), in_hbm(scales), in_hbm(codes))


def forward(msg, gate, up, down):
    return own(
        forward_kernel, "expert_forward", (MSG, HID, HID), [ROWS_SCRATCH, vmem((ROWS, H))],
        14, (15 * 10**9, 10**7), [ON_CHIP] * 4, (ON_CHIP,) * 3,
    )(on_chip(msg), on_chip(gate), on_chip(up), on_chip(down))


def backward(msg, silu, slope, gate, up, down):
    return own(
        backward_kernel, "expert_backward", MSG, [ROWS_SCRATCH, vmem((ROWS, H)), vmem((ROWS, H))],
        14, (15 * 10**9, 3 * 10**7), [ON_CHIP] * 6, ON_CHIP,
    )(on_chip(msg), on_chip(silu), on_chip(slope), on_chip(gate), on_chip(up), on_chip(down))


def combine(msg, mix, spread, teacher, ids, scores):
    return own(
        combine_kernel, "combine", (TOK_HBM, struct((K, T), F32), MSG),
        [ROWS_SCRATCH, vmem((T, D)), vmem((ROWS, LANE), F32), copy_sems(4)],
        14, (60 * 10**9, 10**7), [ON_CHIP] * 6, (IN_HBM, ON_CHIP, ON_CHIP),
    )(on_chip(msg), on_chip(mix), on_chip(spread), on_chip(teacher), on_chip(ids), on_chip(scores))


def gather(msg, sums):
    return own(
        gather_kernel, "gather_tokens", TOK_HBM, [ROWS_SCRATCH, vmem((T, D)), copy_sems(4)],
        12, (2 * 10**9, 6 * 10**6), [ON_CHIP] * 2, IN_HBM,
    )(on_chip(msg), on_chip(sums))


def exchange(msg):
    return lax.all_to_all(msg, ("group", "local"), split_axis=0, concat_axis=0, tiled=True)


def per_device(token_codes, block_scales, route_scores, expert_ids, w_gate, w_up, w_down, teacher):
    ids = expert_ids.T
    scores = route_scores.T
    gate, up, down = w_gate[0], w_up[0], w_down[0]
    msg, spread, mix, sums = dispatch(ids, scores, block_scales.T, token_codes)
    out_msg, silu, slope = forward(exchange(msg), gate, up, down)
    student_out, grad_scores, grad_msg = combine(exchange(out_msg), mix, spread, teacher, ids, scores)
    grad_back = backward(exchange(grad_msg), silu, slope, gate, up, down)
    grad_tokens = gather(exchange(grad_back), sums)
    return student_out, grad_tokens, grad_scores.T


def solution(mesh):
    rows = P(("group", "local"), None)
    mats = P(("group", "local"), None, None)
    return jax.shard_map(
        per_device, mesh=mesh, in_specs=(rows, rows, rows, rows, mats, mats, mats, rows),
        out_specs=(rows, rows, rows), check_vma=False,
    )
```

```python
import jax
import jax.numpy as jnp
from jax import lax
from jax.experimental import pallas as pl
from jax.experimental.pallas import tpu as pltpu
from jax.sharding import PartitionSpec as P

T = 128
E = 128
D = 3584
H = 1024
K = 4
CAP = 5
LANE = 128
NB = D // LANE
MAIN = 18
TAIL = NB - MAIN
ROWS = CAP * E
MSG_ROWS = 8 * E
MSG_COLS = MAIN * LANE
GP = 32
GR = GP * 8
F32 = jnp.float32
BF = jnp.bfloat16
NT = (((1,), (1,)), ((), ()))
CHUNKS = ((0, 6), (6, 6), (12, 6))
REST = (MAIN, TAIL)
TILES = (REST,) + CHUNKS


def lanes_of(chunk):
    return slice(chunk[0] * LANE, (chunk[0] + chunk[1]) * LANE)


def cell_of(slot, block):
    index = slot * TAIL + block
    return 5 + index // MAIN, index % MAIN


CELLS = {cell_of(s, b): (s, b) for s in range(CAP) for b in range(TAIL)}


def iota(shape, dim):
    return lax.broadcasted_iota(jnp.int32, shape, dim)


def one_hot(cond):
    return jnp.where(cond, 1.0, 0.0).astype(BF)


def perm_unpack():
    r = iota((GR, GR), 0)
    return one_hot(iota((GR, GR), 1) == (r % GP) * 8 + r // GP)


def perm_pack():
    r = iota((GR, GR), 0)
    return one_hot(iota((GR, GR), 1) == (r % 8) * GP + r // 8)


def unpack(msg_ref, rows_ref, perm, chunk):
    first, count = chunk
    lanes = lanes_of(chunk)
    for g in range(E // GP):
        moved = jnp.dot(perm, msg_ref[g * GR:(g + 1) * GR, lanes], preferred_element_type=F32).astype(BF)
        for s in range(CAP):
            rows_ref[s * E + g * GP:s * E + (g + 1) * GP, lanes] = moved[s * GP:(s + 1) * GP]
        for q in range(5, 8):
            for c in range(first, first + count):
                if (q, c) in CELLS:
                    s, b = CELLS[q, c]
                    rows_ref[s * E + g * GP:s * E + (g + 1) * GP, lanes_of((MAIN + b, 1))] = (
                        moved[q * GP:(q + 1) * GP, lanes_of((c - first, 1))]
                    )


def pack(rows_ref, msg_ref, perm, chunk):
    first, count = chunk
    lanes = lanes_of(chunk)
    blank = jnp.zeros((GP, LANE), BF)
    for g in range(E // GP):
        parts = [rows_ref[s * E + g * GP:s * E + (g + 1) * GP, lanes] for s in range(CAP)]
        for q in range(5, 8):
            cells = []
            for c in range(first, first + count):
                if (q, c) in CELLS:
                    s, b = CELLS[q, c]
                    cells.append(rows_ref[s * E + g * GP:s * E + (g + 1) * GP, lanes_of((MAIN + b, 1))])
                else:
                    cells.append(blank)
            parts.append(jnp.concatenate(cells, axis=1))
        stacked = jnp.concatenate(parts, axis=0)
        msg_ref[g * GR:(g + 1) * GR, lanes] = jnp.dot(perm, stacked, preferred_element_type=F32).astype(BF)


class Copies:
    def __init__(self, sems):
        self.sems = sems
        self.used = 0

    def start(self, source, target):
        copy = pltpu.make_async_copy(source, target, self.sems.at[self.used])
        self.used += 1
        copy.start()
        return copy


def wait_all(copies):
    for copy in copies:
        copy.wait()


def slots_of(ids):
    expert = iota((E, T), 0)
    hits = [jnp.where(ids[k:k + 1, :] == expert, 1.0, 0.0) for k in range(K)]
    hit = hits[0] + hits[1] + hits[2] + hits[3]
    earlier = one_hot(iota((T, T), 0) < iota((T, T), 1))
    before = jnp.dot(hit.astype(BF), earlier, preferred_element_type=F32)
    return hits, hit, before


def gates_of(scores):
    sigma = jax.nn.sigmoid(scores)
    total = jnp.sum(sigma, axis=0, keepdims=True)
    return sigma, total


def dispatch_kernel(
    ids_hbm, scores_hbm, scales_hbm, codes_hbm, msg_ref, spread_ref, mix_ref, sum_ref,
    ids, scores, scales, codes, rows, sems,
):
    copies = Copies(sems)
    ids_copy = copies.start(ids_hbm, ids)
    scales_copy = copies.start(scales_hbm, scales.at[0:NB, :])
    scores_copy = copies.start(scores_hbm, scores)
    code_copies = [copies.start(codes_hbm.at[:, lanes_of(t)], codes.at[:, lanes_of(t)]) for t in TILES]
    perm = perm_pack()
    ids_copy.wait()
    hits, hit, before = slots_of(ids[...])
    here = [(hit > 0.5) & (before == float(s)) for s in range(CAP)]
    pick = jnp.concatenate([one_hot(h) for h in here], axis=0)
    scales_copy.wait()
    scale = scales[...].T
    for tile, copy in zip(TILES, code_copies):
        copy.wait()
        for j in range(tile[0], tile[0] + tile[1]):
            lanes = lanes_of((j, 1))
            codes[:, lanes] = (codes[:, lanes].astype(F32) * scale[:, j:j + 1]).astype(BF)
        lanes = lanes_of(tile)
        rows[:, lanes] = jnp.dot(pick, codes[:, lanes], preferred_element_type=F32).astype(BF)
        if tile is not REST:
            pack(rows, msg_ref, perm, tile)
    scores_copy.wait()
    sigma, total = gates_of(scores[...])
    weight = (2.5 * sigma / total).astype(BF).astype(F32)
    weighted = hits[0] * weight[0:1]
    for k in range(1, K):
        weighted = weighted + hits[k] * weight[k:k + 1]
    for s in range(CAP):
        part = slice(s * E, (s + 1) * E)
        spread = jnp.where(here[s], weighted, 0.0)
        spread_ref[part, :] = spread.astype(BF)
        mix_ref[:, part] = spread.T.astype(BF)
        sum_ref[:, part] = jnp.where(here[s], 1.0, 0.0).T.astype(BF)


def forward_kernel(msg_ref, gate_ref, up_ref, down_ref, out_ref, silu_ref, slope_ref, rows, active):
    perm = perm_unpack()
    for chunk in CHUNKS:
        unpack(msg_ref, rows, perm, chunk)
    for n in range(0, H, 256):
        lanes = slice(n, n + 256)
        pre_gate = jnp.dot(rows[...], gate_ref[:, lanes], preferred_element_type=F32)
        pre_up = jnp.dot(rows[...], up_ref[:, lanes], preferred_element_type=F32)
        sig = jax.nn.sigmoid(pre_gate)
        silu = pre_gate * sig
        active[:, lanes] = (silu * pre_up).astype(BF)
        silu_ref[:, lanes] = silu.astype(BF)
        slope_ref[:, lanes] = (pre_up * (sig * (1.0 + pre_gate * (1.0 - sig)))).astype(BF)
    perm = perm_pack()
    for tile in TILES:
        lanes = lanes_of(tile)
        rows[:, lanes] = jnp.dot(active[...], down_ref[:, lanes], preferred_element_type=F32).astype(BF)
        if tile is not REST:
            pack(rows, out_ref, perm, tile)


def backward_kernel(msg_ref, silu_ref, slope_ref, gate_ref, up_ref, down_ref, out_ref, rows, d_gate, d_up):
    perm = perm_unpack()
    for chunk in CHUNKS:
        unpack(msg_ref, rows, perm, chunk)
    for n in range(0, H, 256):
        lanes = slice(n, n + 256)
        grad_act = lax.dot_general(rows[...], down_ref[lanes, :], NT, preferred_element_type=F32)
        d_up[:, lanes] = (grad_act * silu_ref[:, lanes].astype(F32)).astype(BF)
        d_gate[:, lanes] = (grad_act * slope_ref[:, lanes].astype(F32)).astype(BF)
    perm = perm_pack()
    for tile in TILES:
        lanes = lanes_of(tile)
        summed = lax.dot_general(d_gate[...], gate_ref[lanes, :], NT, preferred_element_type=F32)
        summed = summed + lax.dot_general(d_up[...], up_ref[lanes, :], NT, preferred_element_type=F32)
        rows[:, lanes] = summed.astype(BF)
        if tile is not REST:
            pack(rows, out_ref, perm, tile)


def combine_kernel(
    msg_ref, mix_ref, spread_ref, teacher_ref, ids_ref, scores_ref, student_hbm, grad_scores_ref, out_ref,
    rows, student, inner, sems,
):
    copies = Copies(sems)
    perm = perm_unpack()
    for chunk in CHUNKS:
        unpack(msg_ref, rows, perm, chunk)
    perm = perm_pack()
    sent = []
    for tile in TILES:
        lanes = lanes_of(tile)
        mixed = jnp.dot(mix_ref[...], rows[:, lanes], preferred_element_type=F32).astype(BF)
        student[:, lanes] = mixed
        sent.append(copies.start(student.at[:, lanes], student_hbm.at[:, lanes]))
        upstream = (mixed.astype(F32) - teacher_ref[:, lanes].astype(F32)).astype(BF)
        grad_out = jnp.dot(spread_ref[...], upstream, preferred_element_type=F32)
        product = grad_out * rows[:, lanes].astype(F32)
        partial = product[:, 0:LANE]
        for j in range(1, tile[1]):
            partial = partial + product[:, lanes_of((j, 1))]
        inner[...] = partial if tile is REST else inner[...] + partial
        rows[:, lanes] = grad_out.astype(BF)
        if tile is not REST:
            pack(rows, out_ref, perm, tile)
    slot_inner = jnp.sum(inner[...], axis=1, keepdims=True)
    hits, hit, before = slots_of(ids_ref[...])
    by_expert = jnp.zeros((E, T), F32)
    for s in range(CAP):
        here = (hit > 0.5) & (before == float(s))
        by_expert = by_expert + jnp.where(here, slot_inner[s * E:(s + 1) * E], 0.0)
    sigma, total = gates_of(scores_ref[...])
    weight = (2.5 * sigma / total).astype(BF).astype(F32)
    weighted_inner = jnp.concatenate(
        [jnp.sum(hits[k] * by_expert, axis=0, keepdims=True) for k in range(K)], axis=0
    )
    grad_w = weighted_inner / weight
    inner_sum = jnp.sum(grad_w * sigma, axis=0, keepdims=True)
    grad_scores_ref[...] = 2.5 * sigma * (1.0 - sigma) * (grad_w / total - inner_sum / (total * total))
    wait_all(sent)


def gather_kernel(msg_ref, sum_ref, out_hbm, rows, out, sems):
    copies = Copies(sems)
    perm = perm_unpack()
    sent = []
    for chunk in CHUNKS:
        unpack(msg_ref, rows, perm, chunk)
        tiles = (REST, chunk) if chunk is CHUNKS[-1] else (chunk,)
        for tile in tiles:
            lanes = lanes_of(tile)
            out[:, lanes] = jnp.dot(sum_ref[...], rows[:, lanes], preferred_element_type=F32).astype(BF)
            sent.append(copies.start(out.at[:, lanes], out_hbm.at[:, lanes]))
    wait_all(sent)


def struct(shape, dtype=BF):
    return jax.ShapeDtypeStruct(shape, dtype)


def vmem(shape, dtype=BF):
    return pltpu.VMEM(shape, dtype)


MSG = struct((MSG_ROWS, MSG_COLS))
ROWS_SCRATCH = vmem((ROWS, D))
ON_CHIP = pl.BlockSpec(memory_space=pltpu.VMEM)
IN_HBM = pl.BlockSpec(memory_space=pltpu.HBM)


def on_chip(array):
    return pltpu.with_memory_space_constraint(array, pltpu.VMEM)


def in_hbm(array):
    return pltpu.with_memory_space_constraint(array, pltpu.HBM)


def own(kernel, name, outs, scratch, limit, estimate, in_specs, out_specs):
    return pl.pallas_call(
        kernel, name=name, out_shape=outs, in_specs=in_specs, out_specs=out_specs, scratch_shapes=scratch,
        compiler_params=pltpu.CompilerParams(vmem_limit_bytes=limit * 2**20),
        cost_estimate=pl.CostEstimate(flops=estimate[0], bytes_accessed=estimate[1], transcendentals=0),
    )


def copy_sems(count):
    return pltpu.SemaphoreType.DMA((count,))


HID = struct((ROWS, H))
TOK_HBM = pltpu.HBM((T, D), BF)


def dispatch(ids, scores, scales, codes):
    return own(
        dispatch_kernel, "dispatch", (MSG, struct((ROWS, T)), struct((T, ROWS)), struct((T, ROWS))),
        [vmem((K, T), jnp.int32), vmem((K, T), F32), vmem((LANE, T), F32), vmem((T, D)), ROWS_SCRATCH, copy_sems(7)],
        9, (60 * 10**9, 6 * 10**6), [IN_HBM] * 4, (ON_CHIP,) * 4,
    )(in_hbm(ids), in_hbm(scores), in_hbm(scales), in_hbm(codes))


def forward(msg, gate, up, down):
    return own(
        forward_kernel, "expert_forward", (MSG, HID, HID), [ROWS_SCRATCH, vmem((ROWS, H))],
        9, (15 * 10**9, 10**7), [ON_CHIP] * 4, (ON_CHIP,) * 3,
    )(on_chip(msg), on_chip(gate), on_chip(up), on_chip(down))


def backward(msg, silu, slope, gate, up, down):
    return own(
        backward_kernel, "expert_backward", MSG, [ROWS_SCRATCH, vmem((ROWS, H)), vmem((ROWS, H))],
        11, (15 * 10**9, 3 * 10**7), [ON_CHIP] * 6, ON_CHIP,
    )(on_chip(msg), on_chip(silu), on_chip(slope), on_chip(gate), on_chip(up), on_chip(down))


def combine(msg, mix, spread, teacher, ids, scores):
    return own(
        combine_kernel, "combine", (TOK_HBM, struct((K, T), F32), MSG),
        [ROWS_SCRATCH, vmem((T, D)), vmem((ROWS, LANE), F32), copy_sems(4)],
        9, (60 * 10**9, 10**7), [ON_CHIP] * 6, (IN_HBM, ON_CHIP, ON_CHIP),
    )(on_chip(msg), on_chip(mix), on_chip(spread), on_chip(teacher), on_chip(ids), on_chip(scores))


def gather(msg, sums):
    return own(
        gather_kernel, "gather_tokens", TOK_HBM, [ROWS_SCRATCH, vmem((T, D)), copy_sems(4)],
        8, (2 * 10**9, 6 * 10**6), [ON_CHIP] * 2, IN_HBM,
    )(on_chip(msg), on_chip(sums))


def exchange(msg):
    return lax.all_to_all(msg, ("group", "local"), split_axis=0, concat_axis=0, tiled=True)


def per_device(token_codes, block_scales, route_scores, expert_ids, w_gate, w_up, w_down, teacher):
    ids = expert_ids.T
    scores = route_scores.T
    gate, up, down = w_gate[0], w_up[0], w_down[0]
    msg, spread, mix, sums = dispatch(ids, scores, block_scales.T, token_codes)
    out_msg, silu, slope = forward(exchange(msg), gate, up, down)
    student_out, grad_scores, grad_msg = combine(exchange(out_msg), mix, spread, teacher, ids, scores)
    grad_back = backward(exchange(grad_msg), silu, slope, gate, up, down)
    grad_tokens = gather(exchange(grad_back), sums)
    return student_out, grad_tokens, grad_scores.T


def solution(mesh):
    rows = P(("group", "local"), None)
    mats = P(("group", "local"), None, None)
    return jax.shard_map(
        per_device, mesh=mesh, in_specs=(rows, rows, rows, rows, mats, mats, mats, rows),
        out_specs=(rows, rows, rows), check_vma=False,
    )
```

```python
import jax
import jax.numpy as jnp
from jax import lax
from jax.experimental import pallas as pl
from jax.experimental.pallas import tpu as pltpu
from jax.sharding import PartitionSpec as P

T = 128
E = 128
D = 3584
H = 1024
K = 4
CAP = 5
LANE = 128
NB = D // LANE
ROWS = CAP * E
LINES = CAP - 1
QUART = NB // LINES
MSG_COLS = (NB + QUART) * LANE
GP = 64
GR = GP * LINES
F32 = jnp.float32
BF = jnp.bfloat16
NT = (((1,), (1,)), ((), ()))
TILES = ((0, 10), (10, 10), (20, 8))
LAST = (NB, QUART)


def lanes_of(chunk):
    return slice(chunk[0] * LANE, (chunk[0] + chunk[1]) * LANE)


def iota(shape, dim):
    return lax.broadcasted_iota(jnp.int32, shape, dim)


def one_hot(cond):
    return jnp.where(cond, 1.0, 0.0).astype(BF)


def perm_unpack():
    r = iota((GR, GR), 0)
    return one_hot(iota((GR, GR), 1) == (r % GP) * LINES + r // GP)


def perm_pack():
    r = iota((GR, GR), 0)
    return one_hot(iota((GR, GR), 1) == (r % LINES) * GP + r // LINES)


def slot_rows(slot, g):
    return slice(slot * E + g * GP, slot * E + (g + 1) * GP)


def unpack(msg_ref, rows_ref, perm, chunk):
    lines = msg_ref.reshape(E * LINES, MSG_COLS)
    lanes = lanes_of(chunk)
    for g in range(E // GP):
        moved = jnp.dot(perm, lines[g * GR:(g + 1) * GR, lanes], preferred_element_type=F32).astype(BF)
        for q in range(LINES):
            line = moved[q * GP:(q + 1) * GP]
            if chunk is LAST:
                rows_ref[slot_rows(LINES, g), lanes_of((q * QUART, QUART))] = line
            else:
                rows_ref[slot_rows(q, g), lanes] = line


def unpack_all(msg_ref, rows_ref):
    perm = perm_unpack()
    for chunk in (LAST,) + TILES:
        unpack(msg_ref, rows_ref, perm, chunk)


def pack(rows_ref, msg_ref, perm, chunk):
    lines = msg_ref.reshape(E * LINES, MSG_COLS)
    lanes = lanes_of(chunk)
    for g in range(E // GP):
        if chunk is LAST:
            parts = [rows_ref[slot_rows(LINES, g), lanes_of((q * QUART, QUART))] for q in range(LINES)]
        else:
            parts = [rows_ref[slot_rows(q, g), lanes] for q in range(LINES)]
        stacked = jnp.concatenate(parts, axis=0)
        lines[g * GR:(g + 1) * GR, lanes] = jnp.dot(perm, stacked, preferred_element_type=F32).astype(BF)


class Copies:
    def __init__(self, sems):
        self.sems = sems
        self.used = 0

    def start(self, source, target):
        copy = pltpu.make_async_copy(source, target, self.sems.at[self.used])
        self.used += 1
        copy.start()
        return copy


def wait_all(copies):
    for copy in copies:
        copy.wait()


def slots_of(ids):
    expert = iota((E, T), 0)
    hits = [jnp.where(ids[k:k + 1, :] == expert, 1.0, 0.0) for k in range(K)]
    hit = hits[0] + hits[1] + hits[2] + hits[3]
    earlier = one_hot(iota((T, T), 0) < iota((T, T), 1))
    before = jnp.dot(hit.astype(BF), earlier, preferred_element_type=F32)
    return hits, hit, before


def gates_of(scores):
    sigma = jax.nn.sigmoid(scores)
    total = jnp.sum(sigma, axis=0, keepdims=True)
    return sigma, total


def dispatch_kernel(
    ids_hbm, scores_hbm, scales_hbm, codes_hbm, msg_ref, spread_ref, mix_ref, sum_ref,
    ids, scores, scales, codes, rows, sems,
):
    copies = Copies(sems)
    ids_copy = copies.start(ids_hbm, ids)
    scales_copy = copies.start(scales_hbm, scales.at[0:NB, :])
    scores_copy = copies.start(scores_hbm, scores)
    code_copies = [copies.start(codes_hbm.at[:, lanes_of(t)], codes.at[:, lanes_of(t)]) for t in TILES]
    perm = perm_pack()
    ids_copy.wait()
    hits, hit, before = slots_of(ids[...])
    here = [(hit > 0.5) & (before == float(s)) for s in range(CAP)]
    pick = jnp.concatenate([one_hot(h) for h in here], axis=0)
    scales_copy.wait()
    scale = scales[...].T
    for tile, copy in zip(TILES, code_copies):
        copy.wait()
        for j in range(tile[0], tile[0] + tile[1]):
            lanes = lanes_of((j, 1))
            codes[:, lanes] = (codes[:, lanes].astype(F32) * scale[:, j:j + 1]).astype(BF)
        lanes = lanes_of(tile)
        rows[:, lanes] = jnp.dot(pick, codes[:, lanes], preferred_element_type=F32).astype(BF)
        pack(rows, msg_ref, perm, tile)
    pack(rows, msg_ref, perm, LAST)
    scores_copy.wait()
    sigma, total = gates_of(scores[...])
    weight = (2.5 * sigma / total).astype(BF).astype(F32)
    weighted = hits[0] * weight[0:1]
    for k in range(1, K):
        weighted = weighted + hits[k] * weight[k:k + 1]
    for s in range(CAP):
        part = slice(s * E, (s + 1) * E)
        spread = jnp.where(here[s], weighted, 0.0)
        spread_ref[part, :] = spread.astype(BF)
        mix_ref[:, part] = spread.T.astype(BF)
        sum_ref[:, part] = jnp.where(here[s], 1.0, 0.0).T.astype(BF)


def forward_kernel(msg_ref, gate_ref, up_ref, down_ref, out_ref, silu_ref, slope_ref, rows, active):
    unpack_all(msg_ref, rows)
    for n in range(0, H, 256):
        lanes = slice(n, n + 256)
        pre_gate = jnp.dot(rows[...], gate_ref[:, lanes], preferred_element_type=F32)
        pre_up = jnp.dot(rows[...], up_ref[:, lanes], preferred_element_type=F32)
        sig = jax.nn.sigmoid(pre_gate)
        silu = pre_gate * sig
        active[:, lanes] = (silu * pre_up).astype(BF)
        silu_ref[:, lanes] = silu.astype(BF)
        slope_ref[:, lanes] = (pre_up * (sig * (1.0 + pre_gate * (1.0 - sig)))).astype(BF)
    perm = perm_pack()
    for tile in TILES:
        lanes = lanes_of(tile)
        rows[:, lanes] = jnp.dot(active[...], down_ref[:, lanes], preferred_element_type=F32).astype(BF)
        pack(rows, out_ref, perm, tile)
    pack(rows, out_ref, perm, LAST)


def backward_kernel(msg_ref, silu_ref, slope_ref, gate_ref, up_ref, down_ref, out_ref, rows, d_gate, d_up):
    unpack_all(msg_ref, rows)
    for n in range(0, H, 256):
        lanes = slice(n, n + 256)
        grad_act = lax.dot_general(rows[...], down_ref[lanes, :], NT, preferred_element_type=F32)
        d_up[:, lanes] = (grad_act * silu_ref[:, lanes].astype(F32)).astype(BF)
        d_gate[:, lanes] = (grad_act * slope_ref[:, lanes].astype(F32)).astype(BF)
    perm = perm_pack()
    for tile in TILES:
        lanes = lanes_of(tile)
        summed = lax.dot_general(d_gate[...], gate_ref[lanes, :], NT, preferred_element_type=F32)
        summed = summed + lax.dot_general(d_up[...], up_ref[lanes, :], NT, preferred_element_type=F32)
        rows[:, lanes] = summed.astype(BF)
        pack(rows, out_ref, perm, tile)
    pack(rows, out_ref, perm, LAST)


def combine_kernel(
    msg_ref, mix_ref, spread_ref, teacher_ref, ids_ref, scores_ref, student_hbm, grad_scores_ref, out_ref,
    rows, student, inner, sems,
):
    copies = Copies(sems)
    unpack_all(msg_ref, rows)
    perm = perm_pack()
    sent = []
    for tile in TILES:
        lanes = lanes_of(tile)
        mixed = jnp.dot(mix_ref[...], rows[:, lanes], preferred_element_type=F32).astype(BF)
        student[:, lanes] = mixed
        sent.append(copies.start(student.at[:, lanes], student_hbm.at[:, lanes]))
        upstream = (mixed.astype(F32) - teacher_ref[:, lanes].astype(F32)).astype(BF)
        grad_out = jnp.dot(spread_ref[...], upstream, preferred_element_type=F32)
        product = grad_out * rows[:, lanes].astype(F32)
        partial = product[:, 0:LANE]
        for j in range(1, tile[1]):
            partial = partial + product[:, lanes_of((j, 1))]
        inner[...] = partial if tile is TILES[0] else inner[...] + partial
        rows[:, lanes] = grad_out.astype(BF)
        pack(rows, out_ref, perm, tile)
    pack(rows, out_ref, perm, LAST)
    slot_inner = jnp.sum(inner[...], axis=1, keepdims=True)
    hits, hit, before = slots_of(ids_ref[...])
    by_expert = jnp.zeros((E, T), F32)
    for s in range(CAP):
        here = (hit > 0.5) & (before == float(s))
        by_expert = by_expert + jnp.where(here, slot_inner[s * E:(s + 1) * E], 0.0)
    sigma, total = gates_of(scores_ref[...])
    weight = (2.5 * sigma / total).astype(BF).astype(F32)
    weighted_inner = jnp.concatenate(
        [jnp.sum(hits[k] * by_expert, axis=0, keepdims=True) for k in range(K)], axis=0
    )
    grad_w = weighted_inner / weight
    inner_sum = jnp.sum(grad_w * sigma, axis=0, keepdims=True)
    grad_scores_ref[...] = 2.5 * sigma * (1.0 - sigma) * (grad_w / total - inner_sum / (total * total))
    wait_all(sent)


def gather_kernel(msg_ref, sum_ref, out_hbm, rows, out, sems):
    copies = Copies(sems)
    perm = perm_unpack()
    sent = []
    unpack(msg_ref, rows, perm, LAST)
    for tile in TILES:
        unpack(msg_ref, rows, perm, tile)
        lanes = lanes_of(tile)
        out[:, lanes] = jnp.dot(sum_ref[...], rows[:, lanes], preferred_element_type=F32).astype(BF)
        sent.append(copies.start(out.at[:, lanes], out_hbm.at[:, lanes]))
    wait_all(sent)


def struct(shape, dtype=BF):
    return jax.ShapeDtypeStruct(shape, dtype)


def vmem(shape, dtype=BF):
    return pltpu.VMEM(shape, dtype)


MSG = struct((E, LINES, MSG_COLS))
ROWS_SCRATCH = vmem((ROWS, D))
ON_CHIP = pl.BlockSpec(memory_space=pltpu.VMEM)
IN_HBM = pl.BlockSpec(memory_space=pltpu.HBM)


def on_chip(array):
    return pltpu.with_memory_space_constraint(array, pltpu.VMEM)


def in_hbm(array):
    return pltpu.with_memory_space_constraint(array, pltpu.HBM)


def own(kernel, name, outs, scratch, limit, estimate, in_specs, out_specs):
    return pl.pallas_call(
        kernel, name=name, out_shape=outs, in_specs=in_specs, out_specs=out_specs, scratch_shapes=scratch,
        compiler_params=pltpu.CompilerParams(vmem_limit_bytes=limit * 2**20),
        cost_estimate=pl.CostEstimate(flops=estimate[0], bytes_accessed=estimate[1], transcendentals=0),
    )


def copy_sems(count):
    return pltpu.SemaphoreType.DMA((count,))


HID = struct((ROWS, H))
TOK_HBM = pltpu.HBM((T, D), BF)


def dispatch(ids, scores, scales, codes):
    return own(
        dispatch_kernel, "dispatch", (MSG, struct((ROWS, T)), struct((T, ROWS)), struct((T, ROWS))),
        [vmem((K, T), jnp.int32), vmem((K, T), F32), vmem((LANE, T), F32), vmem((T, D)), ROWS_SCRATCH, copy_sems(6)],
        9, (60 * 10**9, 6 * 10**6), [IN_HBM] * 4, (ON_CHIP,) * 4,
    )(in_hbm(ids), in_hbm(scores), in_hbm(scales), in_hbm(codes))


def forward(msg, gate, up, down):
    return own(
        forward_kernel, "expert_forward", (MSG, HID, HID), [ROWS_SCRATCH, vmem((ROWS, H))],
        9, (15 * 10**9, 10**7), [ON_CHIP] * 4, (ON_CHIP,) * 3,
    )(on_chip(msg), on_chip(gate), on_chip(up), on_chip(down))


def backward(msg, silu, slope, gate, up, down):
    return own(
        backward_kernel, "expert_backward", MSG, [ROWS_SCRATCH, vmem((ROWS, H)), vmem((ROWS, H))],
        11, (15 * 10**9, 3 * 10**7), [ON_CHIP] * 6, ON_CHIP,
    )(on_chip(msg), on_chip(silu), on_chip(slope), on_chip(gate), on_chip(up), on_chip(down))


def combine(msg, mix, spread, teacher, ids, scores):
    return own(
        combine_kernel, "combine", (TOK_HBM, struct((K, T), F32), MSG),
        [ROWS_SCRATCH, vmem((T, D)), vmem((ROWS, LANE), F32), copy_sems(3)],
        9, (60 * 10**9, 10**7), [ON_CHIP] * 6, (IN_HBM, ON_CHIP, ON_CHIP),
    )(on_chip(msg), on_chip(mix), on_chip(spread), on_chip(teacher), on_chip(ids), on_chip(scores))


def gather(msg, sums):
    return own(
        gather_kernel, "gather_tokens", TOK_HBM, [ROWS_SCRATCH, vmem((T, D)), copy_sems(3)],
        8, (2 * 10**9, 6 * 10**6), [ON_CHIP] * 2, IN_HBM,
    )(on_chip(msg), on_chip(sums))


def exchange(msg):
    return lax.all_to_all(msg, ("group", "local"), split_axis=0, concat_axis=0, tiled=True)


def per_device(token_codes, block_scales, route_scores, expert_ids, w_gate, w_up, w_down, teacher):
    ids = expert_ids.T
    scores = route_scores.T
    gate, up, down = w_gate[0], w_up[0], w_down[0]
    msg, spread, mix, sums = dispatch(ids, scores, block_scales.T, token_codes)
    out_msg, silu, slope = forward(exchange(msg), gate, up, down)
    student_out, grad_scores, grad_msg = combine(exchange(out_msg), mix, spread, teacher, ids, scores)
    grad_back = backward(exchange(grad_msg), silu, slope, gate, up, down)
    grad_tokens = gather(exchange(grad_back), sums)
    return student_out, grad_tokens, grad_scores.T


def solution(mesh):
    rows = P(("group", "local"), None)
    mats = P(("group", "local"), None, None)
    return jax.shard_map(
        per_device, mesh=mesh, in_specs=(rows, rows, rows, rows, mats, mats, mats, rows),
        out_specs=(rows, rows, rows), check_vma=False,
    )
```

```python
import jax
import jax.numpy as jnp
from jax import lax
from jax.experimental import pallas as pl
from jax.experimental.pallas import tpu as pltpu
from jax.sharding import PartitionSpec as P

T = 128
E = 128
D = 3584
H = 1024
K = 4
CAP = 5
LANE = 128
NB = D // LANE
ROWS = CAP * E
LINES = CAP - 1
HEAD = E * LINES
QUART = NB // LINES
MSG_COLS = (NB + QUART) * LANE
GP = 64
GR = GP * LINES
F32 = jnp.float32
BF = jnp.bfloat16
NT = (((1,), (1,)), ((), ()))
TILES = ((0, 10), (10, 10), (20, 8))
LAST = (NB, QUART)


def lanes_of(chunk):
    return slice(chunk[0] * LANE, (chunk[0] + chunk[1]) * LANE)


def iota(shape, dim):
    return lax.broadcasted_iota(jnp.int32, shape, dim)


def one_hot(cond):
    return jnp.where(cond, 1.0, 0.0).astype(BF)


def perm_unpack():
    r = iota((GR, GR), 0)
    return one_hot(iota((GR, GR), 1) == (r % GP) * LINES + r // GP)


def perm_pack():
    r = iota((GR, GR), 0)
    return one_hot(iota((GR, GR), 1) == (r % LINES) * GP + r // LINES)


def lines_of(msg_ref):
    return msg_ref.reshape(HEAD, MSG_COLS)


def unpack_last(msg_ref, last_ref):
    perm = perm_unpack()
    lines = lines_of(msg_ref)
    for g in range(E // GP):
        moved = jnp.dot(perm, lines[g * GR:(g + 1) * GR, lanes_of(LAST)], preferred_element_type=F32).astype(BF)
        for q in range(LINES):
            last_ref[g * GP:(g + 1) * GP, lanes_of((q * QUART, QUART))] = moved[q * GP:(q + 1) * GP]


def unpack(msg_ref, rows_ref):
    unpack_last(msg_ref, rows_ref.at[HEAD:, :])
    lines = lines_of(msg_ref)
    for tile in TILES:
        rows_ref[:HEAD, lanes_of(tile)] = lines[:, lanes_of(tile)]


def put(msg_ref, last_ref, lanes, value):
    lines_of(msg_ref)[:, lanes] = value[:HEAD]
    last_ref[:, lanes] = value[HEAD:]


def pack_last(msg_ref, last_ref):
    perm = perm_pack()
    lines = lines_of(msg_ref)
    for g in range(E // GP):
        parts = [last_ref[g * GP:(g + 1) * GP, lanes_of((q * QUART, QUART))] for q in range(LINES)]
        stacked = jnp.concatenate(parts, axis=0)
        lines[g * GR:(g + 1) * GR, lanes_of(LAST)] = jnp.dot(perm, stacked, preferred_element_type=F32).astype(BF)


class Copies:
    def __init__(self, sems):
        self.sems = sems
        self.used = 0

    def start(self, source, target):
        copy = pltpu.make_async_copy(source, target, self.sems.at[self.used])
        self.used += 1
        copy.start()
        return copy


def wait_all(copies):
    for copy in copies:
        copy.wait()


def slots_of(ids):
    row = iota((ROWS, T), 0)
    expert = jnp.where(row < HEAD, row // LINES, row - HEAD)
    slot = jnp.where(row < HEAD, row % LINES, LINES)
    hits = [jnp.where(ids[k:k + 1, :] == expert, 1.0, 0.0) for k in range(K)]
    hit = hits[0] + hits[1] + hits[2] + hits[3]
    earlier = one_hot(iota((T, T), 0) < iota((T, T), 1))
    before = jnp.dot(hit.astype(BF), earlier, preferred_element_type=F32)
    return hits, (hit > 0.5) & (before == slot.astype(F32))


def gates_of(scores):
    sigma = jax.nn.sigmoid(scores)
    total = jnp.sum(sigma, axis=0, keepdims=True)
    return sigma, total


def dispatch_kernel(
    ids_hbm, scores_hbm, scales_hbm, codes_hbm, msg_ref, spread_ref, mix_ref, sum_ref,
    ids, scores, scales, codes, last, sems,
):
    copies = Copies(sems)
    ids_copy = copies.start(ids_hbm, ids)
    scales_copy = copies.start(scales_hbm, scales.at[0:NB, :])
    scores_copy = copies.start(scores_hbm, scores)
    code_copies = [copies.start(codes_hbm.at[:, lanes_of(t)], codes.at[:, lanes_of(t)]) for t in TILES]
    ids_copy.wait()
    hits, here = slots_of(ids[...])
    pick = one_hot(here)
    scales_copy.wait()
    scale = scales[...].T
    for tile, copy in zip(TILES, code_copies):
        copy.wait()
        for j in range(tile[0], tile[0] + tile[1]):
            lanes = lanes_of((j, 1))
            codes[:, lanes] = (codes[:, lanes].astype(F32) * scale[:, j:j + 1]).astype(BF)
        lanes = lanes_of(tile)
        put(msg_ref, last, lanes, jnp.dot(pick, codes[:, lanes], preferred_element_type=F32).astype(BF))
    pack_last(msg_ref, last)
    scores_copy.wait()
    sigma, total = gates_of(scores[...])
    weight = (2.5 * sigma / total).astype(BF).astype(F32)
    weighted = hits[0] * weight[0:1]
    for k in range(1, K):
        weighted = weighted + hits[k] * weight[k:k + 1]
    spread = jnp.where(here, weighted, 0.0)
    held = jnp.where(here, 1.0, 0.0)
    spread_ref[...] = spread.astype(BF)
    for n in range(0, ROWS, T):
        mix_ref[:, n:n + T] = spread[n:n + T].T.astype(BF)
        sum_ref[:, n:n + T] = held[n:n + T].T.astype(BF)


def forward_kernel(msg_ref, gate_ref, up_ref, down_ref, out_ref, silu_ref, slope_ref, rows, active):
    unpack(msg_ref, rows)
    for n in range(0, H, 256):
        lanes = slice(n, n + 256)
        pre_gate = jnp.dot(rows[...], gate_ref[:, lanes], preferred_element_type=F32)
        pre_up = jnp.dot(rows[...], up_ref[:, lanes], preferred_element_type=F32)
        sig = jax.nn.sigmoid(pre_gate)
        silu = pre_gate * sig
        active[:, lanes] = (silu * pre_up).astype(BF)
        silu_ref[:, lanes] = silu.astype(BF)
        slope_ref[:, lanes] = (pre_up * (sig * (1.0 + pre_gate * (1.0 - sig)))).astype(BF)
    last = rows.at[HEAD:, :]
    for tile in TILES:
        lanes = lanes_of(tile)
        put(out_ref, last, lanes, jnp.dot(active[...], down_ref[:, lanes], preferred_element_type=F32).astype(BF))
    pack_last(out_ref, last)


def backward_kernel(msg_ref, silu_ref, slope_ref, gate_ref, up_ref, down_ref, out_ref, rows, d_gate, d_up):
    unpack(msg_ref, rows)
    for n in range(0, H, 256):
        lanes = slice(n, n + 256)
        grad_act = lax.dot_general(rows[...], down_ref[lanes, :], NT, preferred_element_type=F32)
        d_up[:, lanes] = (grad_act * silu_ref[:, lanes].astype(F32)).astype(BF)
        d_gate[:, lanes] = (grad_act * slope_ref[:, lanes].astype(F32)).astype(BF)
    last = rows.at[HEAD:, :]
    for tile in TILES:
        lanes = lanes_of(tile)
        summed = lax.dot_general(d_gate[...], gate_ref[lanes, :], NT, preferred_element_type=F32)
        summed = summed + lax.dot_general(d_up[...], up_ref[lanes, :], NT, preferred_element_type=F32)
        put(out_ref, last, lanes, summed.astype(BF))
    pack_last(out_ref, last)


def summed_rows(table_ref, lines, last, lanes):
    head = jnp.dot(table_ref[:, :HEAD], lines[:, lanes], preferred_element_type=F32)
    return head + jnp.dot(table_ref[:, HEAD:], last[:, lanes], preferred_element_type=F32)


def combine_kernel(
    msg_ref, mix_ref, spread_ref, teacher_ref, ids_ref, scores_ref, student_hbm, grad_scores_ref, out_ref,
    last, sent_last, student, inner, sems,
):
    copies = Copies(sems)
    unpack_last(msg_ref, last)
    lines = lines_of(msg_ref)
    sent = []
    for tile in TILES:
        lanes = lanes_of(tile)
        mixed = summed_rows(mix_ref, lines, last, lanes).astype(BF)
        student[:, lanes] = mixed
        sent.append(copies.start(student.at[:, lanes], student_hbm.at[:, lanes]))
        upstream = (mixed.astype(F32) - teacher_ref[:, lanes].astype(F32)).astype(BF)
        grad_out = jnp.dot(spread_ref[...], upstream, preferred_element_type=F32)
        for part, held in ((slice(0, HEAD), lines), (slice(HEAD, ROWS), last)):
            product = grad_out[part] * held[:, lanes].astype(F32)
            partial = product[:, 0:LANE]
            for j in range(1, tile[1]):
                partial = partial + product[:, lanes_of((j, 1))]
            inner[part, :] = partial if tile is TILES[0] else inner[part, :] + partial
        put(out_ref, sent_last, lanes, grad_out.astype(BF))
    pack_last(out_ref, sent_last)
    hits, here = slots_of(ids_ref[...])
    slot_inner = jnp.where(here, jnp.sum(inner[...], axis=1, keepdims=True), 0.0)
    sigma, total = gates_of(scores_ref[...])
    weight = (2.5 * sigma / total).astype(BF).astype(F32)
    weighted_inner = jnp.concatenate(
        [jnp.sum(hits[k] * slot_inner, axis=0, keepdims=True) for k in range(K)], axis=0
    )
    grad_w = weighted_inner / weight
    inner_sum = jnp.sum(grad_w * sigma, axis=0, keepdims=True)
    grad_scores_ref[...] = 2.5 * sigma * (1.0 - sigma) * (grad_w / total - inner_sum / (total * total))
    wait_all(sent)


def gather_kernel(msg_ref, sum_ref, out_hbm, last, out, sems):
    copies = Copies(sems)
    unpack_last(msg_ref, last)
    lines = lines_of(msg_ref)
    sent = []
    for tile in TILES:
        lanes = lanes_of(tile)
        out[:, lanes] = summed_rows(sum_ref, lines, last, lanes).astype(BF)
        sent.append(copies.start(out.at[:, lanes], out_hbm.at[:, lanes]))
    wait_all(sent)


def struct(shape, dtype=BF):
    return jax.ShapeDtypeStruct(shape, dtype)


def vmem(shape, dtype=BF):
    return pltpu.VMEM(shape, dtype)


MSG = struct((E, LINES, MSG_COLS))
ROWS_SCRATCH = vmem((ROWS, D))
LAST_SCRATCH = vmem((E, D))
ON_CHIP = pl.BlockSpec(memory_space=pltpu.VMEM)
IN_HBM = pl.BlockSpec(memory_space=pltpu.HBM)


def on_chip(array):
    return pltpu.with_memory_space_constraint(array, pltpu.VMEM)


def in_hbm(array):
    return pltpu.with_memory_space_constraint(array, pltpu.HBM)


def own(kernel, name, outs, scratch, limit, estimate, in_specs, out_specs):
    return pl.pallas_call(
        kernel, name=name, out_shape=outs, in_specs=in_specs, out_specs=out_specs, scratch_shapes=scratch,
        compiler_params=pltpu.CompilerParams(vmem_limit_bytes=limit * 2**20),
        cost_estimate=pl.CostEstimate(flops=estimate[0], bytes_accessed=estimate[1], transcendentals=0),
    )


def copy_sems(count):
    return pltpu.SemaphoreType.DMA((count,))


HID = struct((ROWS, H))
TOK_HBM = pltpu.HBM((T, D), BF)


def dispatch(ids, scores, scales, codes):
    return own(
        dispatch_kernel, "dispatch", (MSG, struct((ROWS, T)), struct((T, ROWS)), struct((T, ROWS))),
        [vmem((K, T), jnp.int32), vmem((K, T), F32), vmem((LANE, T), F32), vmem((T, D)), LAST_SCRATCH, copy_sems(6)],
        9, (60 * 10**9, 6 * 10**6), [IN_HBM] * 4, (ON_CHIP,) * 4,
    )(in_hbm(ids), in_hbm(scores), in_hbm(scales), in_hbm(codes))


def forward(msg, gate, up, down):
    return own(
        forward_kernel, "expert_forward", (MSG, HID, HID), [ROWS_SCRATCH, vmem((ROWS, H))],
        9, (15 * 10**9, 10**7), [ON_CHIP] * 4, (ON_CHIP,) * 3,
    )(on_chip(msg), on_chip(gate), on_chip(up), on_chip(down))


def backward(msg, silu, slope, gate, up, down):
    return own(
        backward_kernel, "expert_backward", MSG, [ROWS_SCRATCH, vmem((ROWS, H)), vmem((ROWS, H))],
        11, (15 * 10**9, 3 * 10**7), [ON_CHIP] * 6, ON_CHIP,
    )(on_chip(msg), on_chip(silu), on_chip(slope), on_chip(gate), on_chip(up), on_chip(down))


def combine(msg, mix, spread, teacher, ids, scores):
    return own(
        combine_kernel, "combine", (TOK_HBM, struct((K, T), F32), MSG),
        [LAST_SCRATCH, LAST_SCRATCH, vmem((T, D)), vmem((ROWS, LANE), F32), copy_sems(3)],
        9, (60 * 10**9, 10**7), [ON_CHIP] * 6, (IN_HBM, ON_CHIP, ON_CHIP),
    )(on_chip(msg), on_chip(mix), on_chip(spread), on_chip(teacher), on_chip(ids), on_chip(scores))


def gather(msg, sums):
    return own(
        gather_kernel, "gather_tokens", TOK_HBM, [LAST_SCRATCH, vmem((T, D)), copy_sems(3)],
        8, (2 * 10**9, 6 * 10**6), [ON_CHIP] * 2, IN_HBM,
    )(on_chip(msg), on_chip(sums))


def exchange(msg):
    return lax.all_to_all(msg, ("group", "local"), split_axis=0, concat_axis=0, tiled=True)


def per_device(token_codes, block_scales, route_scores, expert_ids, w_gate, w_up, w_down, teacher):
    ids = expert_ids.T
    scores = route_scores.T
    gate, up, down = w_gate[0], w_up[0], w_down[0]
    msg, spread, mix, sums = dispatch(ids, scores, block_scales.T, token_codes)
    out_msg, silu, slope = forward(exchange(msg), gate, up, down)
    student_out, grad_scores, grad_msg = combine(exchange(out_msg), mix, spread, teacher, ids, scores)
    grad_back = backward(exchange(grad_msg), silu, slope, gate, up, down)
    grad_tokens = gather(exchange(grad_back), sums)
    return student_out, grad_tokens, grad_scores.T


def solution(mesh):
    rows = P(("group", "local"), None)
    mats = P(("group", "local"), None, None)
    return jax.shard_map(
        per_device, mesh=mesh, in_specs=(rows, rows, rows, rows, mats, mats, mats, rows),
        out_specs=(rows, rows, rows), check_vma=False,
    )
```

```python
import jax
import jax.numpy as jnp
from jax import lax
from jax.experimental import pallas as pl
from jax.experimental.pallas import tpu as pltpu
from jax.sharding import PartitionSpec as P

T = 128
E = 128
D = 3584
H = 1024
K = 4
CAP = 5
LANE = 128
NB = D // LANE
ROWS = CAP * E
LINES = CAP - 1
HEAD = E * LINES
QUART = NB // LINES
MSG_COLS = (NB + QUART) * LANE
GP = 64
GR = GP * LINES
F32 = jnp.float32
BF = jnp.bfloat16
NT = (((1,), (1,)), ((), ()))
TILES = ((0, 10), (10, 10), (20, 8))
LAST = (NB, QUART)


def lanes_of(chunk):
    return slice(chunk[0] * LANE, (chunk[0] + chunk[1]) * LANE)


def iota(shape, dim):
    return lax.broadcasted_iota(jnp.int32, shape, dim)


def one_hot(cond):
    return jnp.where(cond, 1.0, 0.0).astype(BF)


def perm_unpack():
    r = iota((GR, GR), 0)
    return one_hot(iota((GR, GR), 1) == (r % GP) * LINES + r // GP)


def perm_pack():
    r = iota((GR, GR), 0)
    return one_hot(iota((GR, GR), 1) == (r % LINES) * GP + r // LINES)


def lines_of(msg_ref):
    return msg_ref.reshape(HEAD, MSG_COLS)


def unpack_last(msg_ref, last_ref):
    perm = perm_unpack()
    lines = lines_of(msg_ref)
    for g in range(E // GP):
        moved = jnp.dot(perm, lines[g * GR:(g + 1) * GR, lanes_of(LAST)], preferred_element_type=F32).astype(BF)
        for q in range(LINES):
            last_ref[g * GP:(g + 1) * GP, lanes_of((q * QUART, QUART))] = moved[q * GP:(q + 1) * GP]


def unpack(msg_ref, rows_ref):
    unpack_last(msg_ref, rows_ref.at[HEAD:, :])
    lines = lines_of(msg_ref)
    for tile in TILES:
        rows_ref[:HEAD, lanes_of(tile)] = lines[:, lanes_of(tile)]


def put(msg_ref, last_ref, lanes, value):
    lines_of(msg_ref)[:, lanes] = value[:HEAD]
    last_ref[:, lanes] = value[HEAD:]


def pack_last(msg_ref, last_ref):
    perm = perm_pack()
    lines = lines_of(msg_ref)
    for g in range(E // GP):
        parts = [last_ref[g * GP:(g + 1) * GP, lanes_of((q * QUART, QUART))] for q in range(LINES)]
        stacked = jnp.concatenate(parts, axis=0)
        lines[g * GR:(g + 1) * GR, lanes_of(LAST)] = jnp.dot(perm, stacked, preferred_element_type=F32).astype(BF)


class Copies:
    def __init__(self, sems):
        self.sems = sems
        self.used = 0

    def start(self, source, target):
        copy = pltpu.make_async_copy(source, target, self.sems.at[self.used])
        self.used += 1
        copy.start()
        return copy


def wait_all(copies):
    for copy in copies:
        copy.wait()


def slots_of(ids):
    row = iota((ROWS, T), 0)
    expert = jnp.where(row < HEAD, row // LINES, row - HEAD)
    slot = jnp.where(row < HEAD, row % LINES, LINES)
    hits = [jnp.where(ids[k:k + 1, :] == expert, 1.0, 0.0) for k in range(K)]
    hit = hits[0] + hits[1] + hits[2] + hits[3]
    earlier = one_hot(iota((T, T), 0) < iota((T, T), 1))
    before = jnp.dot(hit.astype(BF), earlier, preferred_element_type=F32)
    return hits, (hit > 0.5) & (before == slot.astype(F32))


def gates_of(scores):
    sigma = jax.nn.sigmoid(scores)
    total = jnp.sum(sigma, axis=0, keepdims=True)
    return sigma, total


def dispatch_kernel(
    ids_hbm, scores_hbm, scales_hbm, codes_hbm, msg_ref, spread_ref, mix_ref,
    ids, scores, scales, codes, last, sems,
):
    copies = Copies(sems)
    ids_copy = copies.start(ids_hbm, ids)
    scales_copy = copies.start(scales_hbm, scales.at[0:NB, :])
    scores_copy = copies.start(scores_hbm, scores)
    code_copies = [copies.start(codes_hbm.at[:, lanes_of(t)], codes.at[:, lanes_of(t)]) for t in TILES]
    ids_copy.wait()
    hits, here = slots_of(ids[...])
    pick = one_hot(here)
    scales_copy.wait()
    scale = scales[...].T
    for tile, copy in zip(TILES, code_copies):
        copy.wait()
        for j in range(tile[0], tile[0] + tile[1]):
            lanes = lanes_of((j, 1))
            codes[:, lanes] = (codes[:, lanes].astype(F32) * scale[:, j:j + 1]).astype(BF)
        lanes = lanes_of(tile)
        put(msg_ref, last, lanes, jnp.dot(pick, codes[:, lanes], preferred_element_type=F32).astype(BF))
    pack_last(msg_ref, last)
    scores_copy.wait()
    sigma, total = gates_of(scores[...])
    weight = (2.5 * sigma / total).astype(BF).astype(F32)
    weighted = hits[0] * weight[0:1]
    for k in range(1, K):
        weighted = weighted + hits[k] * weight[k:k + 1]
    spread = jnp.where(here, weighted, 0.0)
    spread_ref[...] = spread.astype(BF)
    for n in range(0, ROWS, T):
        mix_ref[:, n:n + T] = spread[n:n + T].T.astype(BF)


def write_score_grad(inner, ids, scores, grad_scores_ref):
    hits, here = slots_of(ids)
    slot_inner = jnp.where(here, jnp.sum(inner, axis=1, keepdims=True), 0.0)
    sigma, total = gates_of(scores)
    weight = (2.5 * sigma / total).astype(BF).astype(F32)
    weighted_inner = jnp.concatenate(
        [jnp.sum(hits[k] * slot_inner, axis=0, keepdims=True) for k in range(K)], axis=0
    )
    grad_w = weighted_inner / weight
    inner_sum = jnp.sum(grad_w * sigma, axis=0, keepdims=True)
    grad_scores_ref[...] = 2.5 * sigma * (1.0 - sigma) * (grad_w / total - inner_sum / (total * total))


def forward_kernel(msg_ref, gate_ref, up_ref, down_ref, out_ref, silu_ref, slope_ref, rows, active):
    unpack(msg_ref, rows)
    for n in range(0, H, 256):
        lanes = slice(n, n + 256)
        pre_gate = jnp.dot(rows[...], gate_ref[:, lanes], preferred_element_type=F32)
        pre_up = jnp.dot(rows[...], up_ref[:, lanes], preferred_element_type=F32)
        sig = jax.nn.sigmoid(pre_gate)
        silu = pre_gate * sig
        active[:, lanes] = (silu * pre_up).astype(BF)
        silu_ref[:, lanes] = silu.astype(BF)
        slope_ref[:, lanes] = (pre_up * (sig * (1.0 + pre_gate * (1.0 - sig)))).astype(BF)
    last = rows.at[HEAD:, :]
    for tile in TILES:
        lanes = lanes_of(tile)
        put(out_ref, last, lanes, jnp.dot(active[...], down_ref[:, lanes], preferred_element_type=F32).astype(BF))
    pack_last(out_ref, last)


def backward_kernel(
    msg_ref, silu_ref, slope_ref, gate_ref, up_ref, down_ref, inner_ref, ids_ref, scores_ref,
    out_ref, grad_scores_ref, rows, d_gate, d_up,
):
    write_score_grad(inner_ref[...], ids_ref[...], scores_ref[...], grad_scores_ref)
    unpack(msg_ref, rows)
    for n in range(0, H, 256):
        lanes = slice(n, n + 256)
        grad_act = lax.dot_general(rows[...], down_ref[lanes, :], NT, preferred_element_type=F32)
        d_up[:, lanes] = (grad_act * silu_ref[:, lanes].astype(F32)).astype(BF)
        d_gate[:, lanes] = (grad_act * slope_ref[:, lanes].astype(F32)).astype(BF)
    last = rows.at[HEAD:, :]
    for tile in TILES:
        lanes = lanes_of(tile)
        summed = lax.dot_general(d_gate[...], gate_ref[lanes, :], NT, preferred_element_type=F32)
        summed = summed + lax.dot_general(d_up[...], up_ref[lanes, :], NT, preferred_element_type=F32)
        put(out_ref, last, lanes, summed.astype(BF))
    pack_last(out_ref, last)


def summed_rows(table_ref, lines, last, lanes):
    head = jnp.dot(table_ref[:, :HEAD], lines[:, lanes], preferred_element_type=F32)
    return head + jnp.dot(table_ref[:, HEAD:], last[:, lanes], preferred_element_type=F32)


def combine_kernel(
    msg_ref, mix_ref, spread_ref, teacher_ref, student_hbm, inner, out_ref, last, sent_last, student, sems,
):
    copies = Copies(sems)
    unpack_last(msg_ref, last)
    lines = lines_of(msg_ref)
    sent = []
    for tile in TILES:
        lanes = lanes_of(tile)
        mixed = summed_rows(mix_ref, lines, last, lanes).astype(BF)
        student[:, lanes] = mixed
        sent.append(copies.start(student.at[:, lanes], student_hbm.at[:, lanes]))
        upstream = (mixed.astype(F32) - teacher_ref[:, lanes].astype(F32)).astype(BF)
        grad_out = jnp.dot(spread_ref[...], upstream, preferred_element_type=F32)
        for part, held in ((slice(0, HEAD), lines), (slice(HEAD, ROWS), last)):
            product = grad_out[part] * held[:, lanes].astype(F32)
            partial = product[:, 0:LANE]
            for j in range(1, tile[1]):
                partial = partial + product[:, lanes_of((j, 1))]
            inner[part, :] = partial if tile is TILES[0] else inner[part, :] + partial
        put(out_ref, sent_last, lanes, grad_out.astype(BF))
    pack_last(out_ref, sent_last)
    wait_all(sent)


def gather_kernel(msg_ref, mix_ref, out_hbm, last, held, out, sems):
    copies = Copies(sems)
    held[...] = one_hot(mix_ref[...].astype(F32) > 0.0)
    unpack_last(msg_ref, last)
    lines = lines_of(msg_ref)
    sent = []
    for tile in TILES:
        lanes = lanes_of(tile)
        out[:, lanes] = summed_rows(held, lines, last, lanes).astype(BF)
        sent.append(copies.start(out.at[:, lanes], out_hbm.at[:, lanes]))
    wait_all(sent)


def struct(shape, dtype=BF):
    return jax.ShapeDtypeStruct(shape, dtype)


def vmem(shape, dtype=BF):
    return pltpu.VMEM(shape, dtype)


MSG = struct((E, LINES, MSG_COLS))
ROWS_SCRATCH = vmem((ROWS, D))
LAST_SCRATCH = vmem((E, D))
ON_CHIP = pl.BlockSpec(memory_space=pltpu.VMEM)
IN_HBM = pl.BlockSpec(memory_space=pltpu.HBM)


def on_chip(array):
    return pltpu.with_memory_space_constraint(array, pltpu.VMEM)


def in_hbm(array):
    return pltpu.with_memory_space_constraint(array, pltpu.HBM)


def own(kernel, name, outs, scratch, limit, estimate, in_specs, out_specs):
    return pl.pallas_call(
        kernel, name=name, out_shape=outs, in_specs=in_specs, out_specs=out_specs, scratch_shapes=scratch,
        compiler_params=pltpu.CompilerParams(vmem_limit_bytes=limit * 2**20),
        cost_estimate=pl.CostEstimate(flops=estimate[0], bytes_accessed=estimate[1], transcendentals=0),
    )


def copy_sems(count):
    return pltpu.SemaphoreType.DMA((count,))


HID = struct((ROWS, H))
TOK_HBM = pltpu.HBM((T, D), BF)


def dispatch(ids, scores, scales, codes):
    return own(
        dispatch_kernel, "dispatch", (MSG, struct((ROWS, T)), struct((T, ROWS))),
        [vmem((K, T), jnp.int32), vmem((K, T), F32), vmem((LANE, T), F32), vmem((T, D)), LAST_SCRATCH, copy_sems(6)],
        10, (60 * 10**9, 6 * 10**6), [IN_HBM] * 4, (ON_CHIP,) * 3,
    )(in_hbm(ids), in_hbm(scores), in_hbm(scales), in_hbm(codes))


def forward(msg, gate, up, down):
    return own(
        forward_kernel, "expert_forward", (MSG, HID, HID), [ROWS_SCRATCH, vmem((ROWS, H))],
        11, (15 * 10**9, 10**7), [ON_CHIP] * 4, (ON_CHIP,) * 3,
    )(on_chip(msg), on_chip(gate), on_chip(up), on_chip(down))


def backward(msg, silu, slope, gate, up, down, inner, ids, scores):
    return own(
        backward_kernel, "expert_backward", (MSG, struct((K, T), F32)),
        [ROWS_SCRATCH, vmem((ROWS, H)), vmem((ROWS, H))],
        13, (15 * 10**9, 3 * 10**7), [ON_CHIP] * 9, (ON_CHIP,) * 2,
    )(
        on_chip(msg), on_chip(silu), on_chip(slope), on_chip(gate), on_chip(up), on_chip(down),
        on_chip(inner), on_chip(ids), on_chip(scores),
    )


def combine(msg, mix, spread, teacher):
    return own(
        combine_kernel, "combine", (TOK_HBM, struct((ROWS, LANE), F32), MSG),
        [LAST_SCRATCH, LAST_SCRATCH, vmem((T, D)), copy_sems(3)],
        10, (60 * 10**9, 10**7), [ON_CHIP] * 4, (IN_HBM, ON_CHIP, ON_CHIP),
    )(on_chip(msg), on_chip(mix), on_chip(spread), on_chip(teacher))


def gather(msg, mix):
    return own(
        gather_kernel, "gather_tokens", TOK_HBM, [LAST_SCRATCH, vmem((T, ROWS)), vmem((T, D)), copy_sems(3)],
        9, (2 * 10**9, 6 * 10**6), [ON_CHIP] * 2, IN_HBM,
    )(on_chip(msg), on_chip(mix))


def exchange(msg):
    return lax.all_to_all(msg, ("group", "local"), split_axis=0, concat_axis=0, tiled=True)


def per_device(token_codes, block_scales, route_scores, expert_ids, w_gate, w_up, w_down, teacher):
    ids = expert_ids.T
    scores = route_scores.T
    gate, up, down = w_gate[0], w_up[0], w_down[0]
    msg, spread, mix = dispatch(ids, scores, block_scales.T, token_codes)
    out_msg, silu, slope = forward(exchange(msg), gate, up, down)
    student_out, inner, grad_msg = combine(exchange(out_msg), mix, spread, teacher)
    grad_back, grad_scores = backward(exchange(grad_msg), silu, slope, gate, up, down, inner, ids, scores)
    grad_tokens = gather(exchange(grad_back), mix)
    return student_out, grad_tokens, grad_scores.T


def solution(mesh):
    rows = P(("group", "local"), None)
    mats = P(("group", "local"), None, None)
    return jax.shard_map(
        per_device, mesh=mesh, in_specs=(rows, rows, rows, rows, mats, mats, mats, rows),
        out_specs=(rows, rows, rows), check_vma=False,
    )
```

```python
import jax
import jax.numpy as jnp
from jax import lax
from jax.experimental import pallas as pl
from jax.experimental.pallas import tpu as pltpu
from jax.sharding import PartitionSpec as P

T = 128
E = 128
D = 3584
H = 1024
K = 4
CAP = 5
LANE = 128
NB = D // LANE
ROWS = CAP * E
LINES = CAP - 1
HEAD = E * LINES
QUART = NB // LINES
MSG_COLS = (NB + QUART) * LANE
GP = 64
GR = GP * LINES
F32 = jnp.float32
BF = jnp.bfloat16
NT = (((1,), (1,)), ((), ()))
TILES = ((0, 10), (10, 10), (20, 8))
LAST = (NB, QUART)


def lanes_of(chunk):
    return slice(chunk[0] * LANE, (chunk[0] + chunk[1]) * LANE)


def iota(shape, dim):
    return lax.broadcasted_iota(jnp.int32, shape, dim)


def one_hot(cond):
    return jnp.where(cond, 1.0, 0.0).astype(BF)


def perm_unpack():
    r = iota((GR, GR), 0)
    return one_hot(iota((GR, GR), 1) == (r % GP) * LINES + r // GP)


def perm_pack():
    r = iota((GR, GR), 0)
    return one_hot(iota((GR, GR), 1) == (r % LINES) * GP + r // LINES)


def lines_of(msg_ref):
    return msg_ref.reshape(HEAD, MSG_COLS)


def unpack_last(msg_ref, last_ref):
    perm = perm_unpack()
    lines = lines_of(msg_ref)
    for g in range(E // GP):
        moved = jnp.dot(perm, lines[g * GR:(g + 1) * GR, lanes_of(LAST)], preferred_element_type=F32).astype(BF)
        for q in range(LINES):
            last_ref[g * GP:(g + 1) * GP, lanes_of((q * QUART, QUART))] = moved[q * GP:(q + 1) * GP]


def unpack(msg_ref, rows_ref):
    unpack_last(msg_ref, rows_ref.at[HEAD:, :])
    lines = lines_of(msg_ref)
    for tile in TILES:
        rows_ref[:HEAD, lanes_of(tile)] = lines[:, lanes_of(tile)]


def put(msg_ref, last_ref, lanes, value):
    lines_of(msg_ref)[:, lanes] = value[:HEAD]
    last_ref[:, lanes] = value[HEAD:]


def pack_last(msg_ref, last_ref):
    perm = perm_pack()
    lines = lines_of(msg_ref)
    for g in range(E // GP):
        parts = [last_ref[g * GP:(g + 1) * GP, lanes_of((q * QUART, QUART))] for q in range(LINES)]
        stacked = jnp.concatenate(parts, axis=0)
        lines[g * GR:(g + 1) * GR, lanes_of(LAST)] = jnp.dot(perm, stacked, preferred_element_type=F32).astype(BF)


class Copies:
    def __init__(self, sems):
        self.sems = sems
        self.used = 0

    def start(self, source, target):
        copy = pltpu.make_async_copy(source, target, self.sems.at[self.used])
        self.used += 1
        copy.start()
        return copy


def wait_all(copies):
    for copy in copies:
        copy.wait()


def slots_of(ids):
    row = iota((ROWS, T), 0)
    expert = jnp.where(row < HEAD, row // LINES, row - HEAD)
    slot = jnp.where(row < HEAD, row % LINES, LINES)
    hits = [jnp.where(ids[k:k + 1, :] == expert, 1.0, 0.0) for k in range(K)]
    hit = hits[0] + hits[1] + hits[2] + hits[3]
    earlier = one_hot(iota((T, T), 0) < iota((T, T), 1))
    before = jnp.dot(hit.astype(BF), earlier, preferred_element_type=F32)
    return hits, (hit > 0.5) & (before == slot.astype(F32))


def gates_of(scores):
    sigma = jax.nn.sigmoid(scores)
    total = jnp.sum(sigma, axis=0, keepdims=True)
    return sigma, total


def dispatch_kernel(
    ids_hbm, scores_hbm, scales_hbm, codes_hbm, msg_ref, spread_ref, mix_ref,
    ids, scores, scales, codes, last, sems,
):
    copies = Copies(sems)
    ids_copy = copies.start(ids_hbm, ids)
    scales_copy = copies.start(scales_hbm, scales.at[0:NB, :])
    scores_copy = copies.start(scores_hbm, scores)
    code_copies = [copies.start(codes_hbm.at[:, lanes_of(t)], codes.at[:, lanes_of(t)]) for t in TILES]
    ids_copy.wait()
    hits, here = slots_of(ids[...])
    pick = one_hot(here)
    scores_copy.wait()
    sigma, total = gates_of(scores[...])
    weight = (2.5 * sigma / total).astype(BF).astype(F32)
    weighted = hits[0] * weight[0:1]
    for k in range(1, K):
        weighted = weighted + hits[k] * weight[k:k + 1]
    spread = jnp.where(here, weighted, 0.0)
    spread_ref[...] = spread.astype(BF)
    for n in range(0, ROWS, T):
        mix_ref[:, n:n + T] = spread[n:n + T].T.astype(BF)
    scales_copy.wait()
    scale = scales[...].T
    for tile, copy in zip(TILES, code_copies):
        copy.wait()
        for j in range(tile[0], tile[0] + tile[1]):
            lanes = lanes_of((j, 1))
            codes[:, lanes] = (codes[:, lanes].astype(F32) * scale[:, j:j + 1]).astype(BF)
        lanes = lanes_of(tile)
        put(msg_ref, last, lanes, jnp.dot(pick, codes[:, lanes], preferred_element_type=F32).astype(BF))
    pack_last(msg_ref, last)


def write_score_grad(inner, ids, scores, grad_scores_ref):
    hits, here = slots_of(ids)
    slot_inner = jnp.where(here, jnp.sum(inner, axis=1, keepdims=True), 0.0)
    sigma, total = gates_of(scores)
    weight = (2.5 * sigma / total).astype(BF).astype(F32)
    weighted_inner = jnp.concatenate(
        [jnp.sum(hits[k] * slot_inner, axis=0, keepdims=True) for k in range(K)], axis=0
    )
    grad_w = weighted_inner / weight
    inner_sum = jnp.sum(grad_w * sigma, axis=0, keepdims=True)
    grad_scores_ref[...] = 2.5 * sigma * (1.0 - sigma) * (grad_w / total - inner_sum / (total * total))


def forward_kernel(msg_ref, gate_ref, up_ref, down_ref, out_ref, silu_ref, slope_ref, rows, active):
    unpack(msg_ref, rows)
    for n in range(0, H, 256):
        lanes = slice(n, n + 256)
        pre_gate = jnp.dot(rows[...], gate_ref[:, lanes], preferred_element_type=F32)
        pre_up = jnp.dot(rows[...], up_ref[:, lanes], preferred_element_type=F32)
        sig = jax.nn.sigmoid(pre_gate)
        silu = pre_gate * sig
        active[:, lanes] = (silu * pre_up).astype(BF)
        silu_ref[:, lanes] = silu.astype(BF)
        slope_ref[:, lanes] = (pre_up * (sig * (1.0 + pre_gate * (1.0 - sig)))).astype(BF)
    last = rows.at[HEAD:, :]
    for tile in TILES:
        lanes = lanes_of(tile)
        put(out_ref, last, lanes, jnp.dot(active[...], down_ref[:, lanes], preferred_element_type=F32).astype(BF))
    pack_last(out_ref, last)


def backward_kernel(
    msg_ref, silu_ref, slope_ref, gate_ref, up_ref, down_ref, inner_ref, ids_ref, scores_ref,
    out_ref, grad_scores_ref, rows, d_gate, d_up,
):
    write_score_grad(inner_ref[...], ids_ref[...], scores_ref[...], grad_scores_ref)
    unpack(msg_ref, rows)
    for n in range(0, H, 256):
        lanes = slice(n, n + 256)
        grad_act = lax.dot_general(rows[...], down_ref[lanes, :], NT, preferred_element_type=F32)
        d_up[:, lanes] = (grad_act * silu_ref[:, lanes].astype(F32)).astype(BF)
        d_gate[:, lanes] = (grad_act * slope_ref[:, lanes].astype(F32)).astype(BF)
    last = rows.at[HEAD:, :]
    for tile in TILES:
        lanes = lanes_of(tile)
        summed = lax.dot_general(d_gate[...], gate_ref[lanes, :], NT, preferred_element_type=F32)
        summed = summed + lax.dot_general(d_up[...], up_ref[lanes, :], NT, preferred_element_type=F32)
        put(out_ref, last, lanes, summed.astype(BF))
    pack_last(out_ref, last)


def summed_rows(table_ref, lines, last, lanes):
    head = jnp.dot(table_ref[:, :HEAD], lines[:, lanes], preferred_element_type=F32)
    return head + jnp.dot(table_ref[:, HEAD:], last[:, lanes], preferred_element_type=F32)


def combine_kernel(
    msg_ref, mix_ref, spread_ref, teacher_ref, student_hbm, inner, out_ref, last, sent_last, student, sems,
):
    copies = Copies(sems)
    unpack_last(msg_ref, last)
    lines = lines_of(msg_ref)
    sent = []
    for tile in TILES:
        lanes = lanes_of(tile)
        mixed = summed_rows(mix_ref, lines, last, lanes).astype(BF)
        student[:, lanes] = mixed
        sent.append(copies.start(student.at[:, lanes], student_hbm.at[:, lanes]))
        upstream = (mixed.astype(F32) - teacher_ref[:, lanes].astype(F32)).astype(BF)
        grad_out = jnp.dot(spread_ref[...], upstream, preferred_element_type=F32)
        for part, held in ((slice(0, HEAD), lines), (slice(HEAD, ROWS), last)):
            product = grad_out[part] * held[:, lanes].astype(F32)
            partial = product[:, 0:LANE]
            for j in range(1, tile[1]):
                partial = partial + product[:, lanes_of((j, 1))]
            inner[part, :] = partial if tile is TILES[0] else inner[part, :] + partial
        put(out_ref, sent_last, lanes, grad_out.astype(BF))
    pack_last(out_ref, sent_last)
    wait_all(sent)


def gather_kernel(msg_ref, mix_ref, out_hbm, last, held, out, sems):
    copies = Copies(sems)
    held[...] = one_hot(mix_ref[...].astype(F32) > 0.0)
    unpack_last(msg_ref, last)
    lines = lines_of(msg_ref)
    sent = []
    for tile in TILES:
        lanes = lanes_of(tile)
        out[:, lanes] = summed_rows(held, lines, last, lanes).astype(BF)
        sent.append(copies.start(out.at[:, lanes], out_hbm.at[:, lanes]))
    wait_all(sent)


def struct(shape, dtype=BF):
    return jax.ShapeDtypeStruct(shape, dtype)


def vmem(shape, dtype=BF):
    return pltpu.VMEM(shape, dtype)


MSG = struct((E, LINES, MSG_COLS))
ROWS_SCRATCH = vmem((ROWS, D))
LAST_SCRATCH = vmem((E, D))
ON_CHIP = pl.BlockSpec(memory_space=pltpu.VMEM)
IN_HBM = pl.BlockSpec(memory_space=pltpu.HBM)


def on_chip(array):
    return pltpu.with_memory_space_constraint(array, pltpu.VMEM)


def in_hbm(array):
    return pltpu.with_memory_space_constraint(array, pltpu.HBM)


def own(kernel, name, outs, scratch, limit, estimate, in_specs, out_specs):
    return pl.pallas_call(
        kernel, name=name, out_shape=outs, in_specs=in_specs, out_specs=out_specs, scratch_shapes=scratch,
        compiler_params=pltpu.CompilerParams(vmem_limit_bytes=limit * 2**20),
        cost_estimate=pl.CostEstimate(flops=estimate[0], bytes_accessed=estimate[1], transcendentals=0),
    )


def copy_sems(count):
    return pltpu.SemaphoreType.DMA((count,))


HID = struct((ROWS, H))
TOK_HBM = pltpu.HBM((T, D), BF)


def dispatch(ids, scores, scales, codes):
    return own(
        dispatch_kernel, "dispatch", (MSG, struct((ROWS, T)), struct((T, ROWS))),
        [vmem((K, T), jnp.int32), vmem((K, T), F32), vmem((LANE, T), F32), vmem((T, D)), LAST_SCRATCH, copy_sems(6)],
        10, (60 * 10**9, 6 * 10**6), [IN_HBM] * 4, (ON_CHIP,) * 3,
    )(in_hbm(ids), in_hbm(scores), in_hbm(scales), in_hbm(codes))


def forward(msg, gate, up, down):
    return own(
        forward_kernel, "expert_forward", (MSG, HID, HID), [ROWS_SCRATCH, vmem((ROWS, H))],
        11, (15 * 10**9, 10**7), [ON_CHIP] * 4, (ON_CHIP,) * 3,
    )(on_chip(msg), on_chip(gate), on_chip(up), on_chip(down))


def backward(msg, silu, slope, gate, up, down, inner, ids, scores):
    return own(
        backward_kernel, "expert_backward", (MSG, struct((K, T), F32)),
        [ROWS_SCRATCH, vmem((ROWS, H)), vmem((ROWS, H))],
        13, (15 * 10**9, 3 * 10**7), [ON_CHIP] * 9, (ON_CHIP,) * 2,
    )(
        on_chip(msg), on_chip(silu), on_chip(slope), on_chip(gate), on_chip(up), on_chip(down),
        on_chip(inner), on_chip(ids), on_chip(scores),
    )


def combine(msg, mix, spread, teacher):
    return own(
        combine_kernel, "combine", (TOK_HBM, struct((ROWS, LANE), F32), MSG),
        [LAST_SCRATCH, LAST_SCRATCH, vmem((T, D)), copy_sems(3)],
        10, (60 * 10**9, 10**7), [ON_CHIP] * 4, (IN_HBM, ON_CHIP, ON_CHIP),
    )(on_chip(msg), on_chip(mix), on_chip(spread), on_chip(teacher))


def gather(msg, mix):
    return own(
        gather_kernel, "gather_tokens", TOK_HBM, [LAST_SCRATCH, vmem((T, ROWS)), vmem((T, D)), copy_sems(3)],
        9, (2 * 10**9, 6 * 10**6), [ON_CHIP] * 2, IN_HBM,
    )(on_chip(msg), on_chip(mix))


def exchange(msg):
    return lax.all_to_all(msg, ("group", "local"), split_axis=0, concat_axis=0, tiled=True)


def per_device(token_codes, block_scales, route_scores, expert_ids, w_gate, w_up, w_down, teacher):
    ids = expert_ids.T
    scores = route_scores.T
    gate, up, down = w_gate[0], w_up[0], w_down[0]
    msg, spread, mix = dispatch(ids, scores, block_scales.T, token_codes)
    out_msg, silu, slope = forward(exchange(msg), gate, up, down)
    student_out, inner, grad_msg = combine(exchange(out_msg), mix, spread, teacher)
    grad_back, grad_scores = backward(exchange(grad_msg), silu, slope, gate, up, down, inner, ids, scores)
    grad_tokens = gather(exchange(grad_back), mix)
    return student_out, grad_tokens, grad_scores.T


def solution(mesh):
    rows = P(("group", "local"), None)
    mats = P(("group", "local"), None, None)
    return jax.shard_map(
        per_device, mesh=mesh, in_specs=(rows, rows, rows, rows, mats, mats, mats, rows),
        out_specs=(rows, rows, rows), check_vma=False,
    )
```
